32 devices in a mesh: side: 2 (over x), grp: 2 (over core), pts: 8 (over z, y).
Axes of the slice: x: 2, y: 2, z: 4, core: 2. Of those that a mesh axis runs over, the one named last changes fastest.
Arguments:
- fields: bfloat16 [2, 4096, 2048], P('side', ('grp', 'pts')), may hold values from -6 to 6
- point_weight: float32 [2, 4096], P('side', ('grp', 'pts')), may hold values from 0.3 to 3
- start_modes: float32 [2, 32, 4096], P('side', None, ('grp', 'pts')), may hold values from -6 to 6
Outputs:
- modes: float32 [2, 32, 4096], P('side', None, ('grp', 'pts'))
The draws below stay inside these ranges and needn't reach their ends.
All inputs are finite; a program needn't handle non-finite values.
Results may differ from the reference program's by a relative error of at most 0.0085.
Values may be sent and summed in bfloat16 or wider, within the bound.
No kernel may reach another device: no remote copies, remote signals or barrier semaphores. Data moves between devices by JAX's collectives and lax.ppermute only.
A program may use at most 64 MiB of HBM per device.

```python
import math
import jax
import jax.numpy as jnp
from jax import lax

MODES = 32
SAMPLES = 2048
ITERS = 6
POINTS = 4096


def level_of(stream_key, shape, pieces, least, largest):
    loudness = 1.0
    for position, parts in pieces:
        draws = jax.random.uniform(jax.random.fold_in(jax.random.fold_in(stream_key, 6), position), (parts,), jnp.float32, least / len(pieces), largest / len(pieces))
        loudness = loudness * jnp.repeat(jnp.exp(draws), shape[position] // parts).reshape((-1,) + (1,) * (len(shape) - 1 - position))
    return loudness


def normal_values(key, dims, spread, reach, pieces=(), dtype=jnp.bfloat16):
    entries = spread * jax.random.normal(key, dims, jnp.float32)
    if pieces:
        entries = entries * level_of(key, dims, pieces, -0.22, 0.18)
    return jnp.clip(entries, -reach, reach).astype(dtype)


def setup_inputs(seed: int = 0) -> dict:
    splits = jax.random.split(jax.random.key(seed), 4)
    return {
        "fields": normal_values(splits[0], (2, POINTS, SAMPLES), 1.0, 6.0, ((0, 2), (1, 16))),
        "point_weight": jnp.clip(jnp.exp(math.log(3.0) - 2.3025851 * jax.random.uniform(splits[1], (2, POINTS), jnp.float32) ** level_of(splits[1], (2, POINTS), ((0, 2), (1, 16)), -0.2, 0.2)), 0.3, 3.0),
        "start_modes": normal_values(splits[2], (2, MODES, POINTS), 1.0, 6.0, ((0, 2), (2, 16)), jnp.float32),
    }


def project_side(weighted, anomaly):
    return jnp.dot(weighted.astype(jnp.float32), anomaly.astype(jnp.float32), preferred_element_type=jnp.float32)

def map_back(coeffs, anomaly):
    return lax.dot_general(coeffs.astype(jnp.float32), anomaly.astype(jnp.float32), (((1,), (1,)), ((), ())), preferred_element_type=jnp.float32)

def reference(fields, point_weight, start_modes):
    mode_rows = start_modes.astype(jnp.float32)
    for iteration in range(ITERS):
        weighted = (mode_rows * point_weight[:, None, :]).astype(jnp.bfloat16)
        coeffs = jnp.stack([project_side(weighted[0], fields[0]), project_side(weighted[1], fields[1])]).astype(jnp.bfloat16)
        mapped = jnp.stack([map_back(coeffs[1], fields[0]), map_back(coeffs[0], fields[1])])
        mapped = mapped * point_weight[:, None, :] / SAMPLES
        outputs = []
        for side_index in range(2):
            gram_sum = jnp.dot(mapped[side_index].astype(jnp.float32), mapped[side_index].T.astype(jnp.float32), precision=lax.Precision.HIGHEST, preferred_element_type=jnp.float32) / POINTS
            factor = jnp.linalg.cholesky(gram_sum)
            outputs.append(lax.linalg.triangular_solve(factor, mapped[side_index], left_side=True, lower=True))
        mode_rows = jnp.stack(outputs)
    return mode_rows
```

```python
import jax
import jax.numpy as jnp
from jax import lax
from jax.experimental import pallas as pl
from jax.experimental.pallas import tpu as pltpu
from jax.sharding import PartitionSpec as P

ITERS = 6
ROWS, LANES = 8, 128
ALL = ("side", "grp", "pts")
F32, BF16 = jnp.float32, jnp.bfloat16
HIGHEST = lax.Precision.HIGHEST
VMEM = pl.BlockSpec(memory_space=pltpu.VMEM)
SMEM = pl.BlockSpec(memory_space=pltpu.SMEM)


def split3(x):
    high = x.astype(BF16)
    rest = x - high.astype(F32)
    mid = rest.astype(BF16)
    low = (rest - mid.astype(F32)).astype(BF16)
    return jnp.concatenate([high, mid, low], axis=0)


def dot_wide(x, field, contract):
    count = x.shape[0]
    out = lax.dot_general(
        split3(x), field, (((1,), (contract,)), ((), ())), preferred_element_type=F32
    )
    return out[2 * count :] + out[count : 2 * count] + out[:count]


def fold(gram, modes):
    return sum(
        pltpu.roll(gram[g * ROWS : (g + 1) * ROWS], g * modes, 1) if g else gram[:ROWS]
        for g in range(modes // ROWS)
    )


def unfold(tile, modes):
    lane = lax.broadcasted_iota(jnp.int32, (ROWS, LANES), 1)
    parts = [
        pltpu.roll(tile, LANES - g * modes, 1) if g else tile for g in range(modes // ROWS)
    ]
    return jnp.concatenate([jnp.where(lane < modes, part, 0.0) for part in parts], axis=0)


def inverse_factor(gram, modes):
    row = lax.broadcasted_iota(jnp.int32, (modes, LANES), 0)
    lane = lax.broadcasted_iota(jnp.int32, (modes, LANES), 1)
    work = gram + jnp.where(lane == row + modes, 1.0, 0.0)
    for k in range(modes):
        top = work[k : k + 1]
        pivot = top[:, k : k + 1]
        factor = jnp.where(row > k, work[:, k : k + 1] / pivot, 0.0)
        work = work - factor * top
    pivots = jnp.sum(jnp.where(lane == row, work, 0.0), axis=1, keepdims=True)
    inverse = pltpu.roll(work, LANES - modes, 1) / jnp.sqrt(pivots)
    return jnp.where(lane < modes, inverse, 0.0)


def store_tiles(send_ref, projected):
    columns = projected.shape[1] // LANES
    for d in range(send_ref.shape[0]):
        h, j = divmod(d, columns)
        send_ref[d, :ROWS, :] = projected[
            h * ROWS : (h + 1) * ROWS, j * LANES : (j + 1) * LANES
        ]


def first_kernel(weighted_ref, field_ref, send_ref):
    store_tiles(send_ref, dot_wide(weighted_ref[...], field_ref[...], 0))


def reduce_kernel(side_ref, recv_ref, send_ref, *gram_ref, grp, pts):
    side = side_ref[0]
    for s in range(2):
        for c in range(grp):
            first = (s * grp + c) * pts
            total = recv_ref[first, :ROWS, :]
            for p in range(1, pts):
                total = total + recv_ref[first + p, :ROWS, :]
            for p in range(pts):
                send_ref[((1 - s) * grp + c) * pts + p] = total
    if gram_ref:
        first = (1 - side) * (grp * pts)
        total = recv_ref[first, ROWS:, :]
        for p in range(1, pts):
            total = total + recv_ref[first + p, ROWS:, :]
        gram_ref[0][...] = total


def factor_kernel(gram_ref, out_ref, *, modes, points):
    out_ref[...] = inverse_factor(unfold(gram_ref[...], modes) / points, modes)


def back_kernel(recv_ref, field_ref, out_ref):
    columns = field_ref.shape[1] // LANES
    count = recv_ref.shape[0] // columns
    coeffs = jnp.concatenate(
        [
            jnp.concatenate([recv_ref[h * columns + j] for j in range(columns)], axis=1)
            for h in range(count)
        ],
        axis=0,
    )
    out_ref[...] = dot_wide(coeffs, field_ref[...], 1)


def map_kernel(*refs, samples, others, has_factor, last):
    refs = list(refs)
    mapped = refs.pop(0)[...]
    modes, points = mapped.shape
    block = points // (others + 1)
    for k in range(others):
        other = refs.pop(0)[...]
        cut = (others - k) * block
        mapped = mapped + jnp.concatenate([other[:, cut:], other[:, :cut]], axis=1)
    factor = refs.pop(0)[...][:, :modes] if has_factor else None
    weight = refs.pop(0)[...]
    if has_factor:
        mapped = jnp.dot(factor, mapped, precision=HIGHEST, preferred_element_type=F32)
    mapped = mapped * weight / samples
    padded = jnp.concatenate([mapped, jnp.zeros((LANES - modes, points), F32)], axis=0)
    gram = lax.dot_general(
        mapped, padded, (((1,), (1,)), ((), ())), precision=HIGHEST, preferred_element_type=F32
    )
    tile = fold(gram, modes)
    if last:
        out_ref, send_ref = refs
        out_ref[...] = mapped[:, :block]
        for d in range(send_ref.shape[0]):
            send_ref[d] = tile
        return
    field_ref, send_ref = refs
    store_tiles(send_ref, dot_wide(mapped * weight, field_ref[...], 0))
    for d in range(send_ref.shape[0]):
        send_ref[d, ROWS:, :] = tile


def finish_kernel(side_ref, recv_ref, mapped_ref, out_ref, *, grp, pts, points):
    first = side_ref[0] * (grp * pts)
    total = recv_ref[first]
    for p in range(1, pts):
        total = total + recv_ref[first + p]
    mapped = mapped_ref[...]
    modes = mapped.shape[0]
    factor = inverse_factor(unfold(total, modes) / points, modes)[:, :modes]
    out_ref[...] = jnp.dot(factor, mapped, precision=HIGHEST, preferred_element_type=F32)


def call(kernel, outs, *args):
    specs = [SMEM if a.dtype == jnp.int32 else VMEM for a in args]
    many = isinstance(outs, list)
    return pl.pallas_call(
        kernel,
        out_shape=[jax.ShapeDtypeStruct(o, F32) for o in outs] if many
        else jax.ShapeDtypeStruct(outs, F32),
        in_specs=specs,
        out_specs=[VMEM for _ in outs] if many else VMEM,
    )(*args)


def exchange(value):
    return lax.all_to_all(value, ALL, 0, 0)


def shifted(value, shift):
    grp = lax.axis_size("grp")
    return lax.ppermute(value, "grp", [((i + shift) % grp, i) for i in range(grp)])


def body_tiles(fields, point_weight, start_modes):
    local_field, weight, modes0 = fields[0], point_weight, start_modes[0]
    modes, samples = modes0.shape[0], local_field.shape[1]
    grp, pts = lax.axis_size("grp"), lax.axis_size("pts")
    devices = 2 * grp * pts
    total_points = local_field.shape[0] * grp * pts
    columns = samples // grp
    place = lax.axis_index("grp")
    side = lax.axis_index("side").astype(jnp.int32).reshape(1)

    def part(member):
        return lax.dynamic_slice_in_dim(local_field, (member % grp) * columns, columns, 1)

    weighted = modes0 * weight
    blocks, weights, starts = [part(place)], [weight], [weighted]
    for k in range(1, grp):
        blocks.append(shifted(part(place - k), k))
        weights.append(shifted(weight, k))
        starts.append(shifted(weighted, k))
    field = jnp.concatenate(blocks, axis=0)
    weight = jnp.concatenate(weights, axis=1)
    start = jnp.concatenate(starts, axis=1)
    points = weight.shape[1]

    def reduced(recv, has_gram):
        shapes = [(devices, ROWS, LANES)] + [(ROWS, LANES)] * has_gram
        kernel = lambda *refs: reduce_kernel(*refs, grp=grp, pts=pts)
        return call(kernel, shapes, side, recv)

    factor = None
    send = call(first_kernel, (devices, ROWS, LANES), start, field)
    for iteration in range(ITERS):
        has_gram = iteration > 0
        out = reduced(exchange(send), has_gram)
        gathered = exchange(out[0])
        if has_gram:
            kernel = lambda *refs: factor_kernel(*refs, modes=modes, points=total_points)
            factor = call(kernel, (modes, LANES), out[1])
        own = call(back_kernel, (modes, points), gathered, field)
        others = [shifted(own, k) for k in range(1, grp)]
        last = iteration == ITERS - 1
        kernel = lambda *refs: map_kernel(
            *refs, samples=samples, others=grp - 1, has_factor=has_gram, last=last
        )
        given = [own, *others, *([factor] if has_gram else []), weight]
        if last:
            shapes = [(modes, points // grp), (devices, ROWS, LANES)]
            mapped, send = call(kernel, shapes, *given)
        else:
            send = call(kernel, (devices, 2 * ROWS, LANES), *given, field)
    kernel = lambda *refs: finish_kernel(*refs, grp=grp, pts=pts, points=total_points)
    return call(kernel, (modes, points // grp), side, exchange(send), mapped)[None]


def body_sums(fields, point_weight, start_modes):
    local_field, weight, mode_rows = fields[0], point_weight[0], start_modes[0]
    samples = local_field.shape[1]
    total_points = local_field.shape[0] * lax.axis_size("grp") * lax.axis_size("pts")
    for _ in range(ITERS):
        weighted = (mode_rows * weight[None, :]).astype(BF16)
        partial = jnp.dot(weighted, local_field, preferred_element_type=F32)
        coeffs = lax.psum(partial, ("grp", "pts")).astype(BF16)
        partner = lax.ppermute(coeffs, "side", [(0, 1), (1, 0)])
        mapped = lax.dot_general(
            partner, local_field, (((1,), (1,)), ((), ())), preferred_element_type=F32
        )
        mapped = mapped * weight[None, :] / samples
        gram = jnp.dot(mapped, mapped.T, precision=HIGHEST, preferred_element_type=F32)
        gram = lax.psum(gram, ("grp", "pts")) / total_points
        factor = jnp.linalg.cholesky(gram)
        mode_rows = lax.linalg.triangular_solve(factor, mapped, left_side=True, lower=True)
    return mode_rows[None]


def solution(mesh):
    grp, pts = mesh.shape["grp"], mesh.shape["pts"]

    def run(fields, point_weight, start_modes):
        modes, samples = start_modes.shape[1], fields.shape[2]
        tiles = (modes // ROWS) * (samples // (LANES * grp))
        fits = tiles == 2 * grp * pts and 4 * modes == LANES
        placed = (
            P("side", ("grp", "pts"), None),
            P("side", ("grp", "pts")),
            P("side", None, ("grp", "pts")),
        )
        return jax.shard_map(
            body_tiles if fits else body_sums,
            mesh=mesh,
            in_specs=placed,
            out_specs=P("side", None, ("grp", "pts")),
            check_vma=False,
        )(fields, point_weight, start_modes)

    return run
```

```python
import jax
import jax.numpy as jnp
from jax import lax
from jax.experimental import pallas as pl
from jax.experimental.pallas import tpu as pltpu
from jax.sharding import PartitionSpec as P

ITERS = 6
ROWS, LANES = 8, 128
ALL = ("side", "grp", "pts")
F32, BF16 = jnp.float32, jnp.bfloat16
HIGHEST = lax.Precision.HIGHEST
VMEM = pl.BlockSpec(memory_space=pltpu.VMEM)
SMEM = pl.BlockSpec(memory_space=pltpu.SMEM)


def split3(x):
    high = x.astype(BF16)
    rest = x - high.astype(F32)
    mid = rest.astype(BF16)
    low = (rest - mid.astype(F32)).astype(BF16)
    return jnp.concatenate([high, mid, low], axis=0)


def dot_wide(x, field, contract):
    count = x.shape[0]
    out = lax.dot_general(
        split3(x), field, (((1,), (contract,)), ((), ())), preferred_element_type=F32
    )
    return out[2 * count :] + out[count : 2 * count] + out[:count]


def fold(gram, modes):
    return sum(
        pltpu.roll(gram[g * ROWS : (g + 1) * ROWS], g * modes, 1) if g else gram[:ROWS]
        for g in range(modes // ROWS)
    )


def unfold(tile, modes):
    lane = lax.broadcasted_iota(jnp.int32, (ROWS, LANES), 1)
    parts = [
        pltpu.roll(tile, LANES - g * modes, 1) if g else tile for g in range(modes // ROWS)
    ]
    return jnp.concatenate([jnp.where(lane < modes, part, 0.0) for part in parts], axis=0)


def inverse_factor(gram, modes):
    row = lax.broadcasted_iota(jnp.int32, (modes, LANES), 0)
    lane = lax.broadcasted_iota(jnp.int32, (modes, LANES), 1)
    work = gram + jnp.where(lane == row + modes, 1.0, 0.0)
    for k in range(modes):
        top = work[k : k + 1]
        pivot = top[:, k : k + 1]
        factor = jnp.where(row > k, work[:, k : k + 1] / pivot, 0.0)
        work = work - factor * top
    pivots = jnp.sum(jnp.where(lane == row, work, 0.0), axis=1, keepdims=True)
    inverse = pltpu.roll(work, LANES - modes, 1) / jnp.sqrt(pivots)
    return jnp.where(lane < modes, inverse, 0.0)


def store_tiles(send_ref, projected):
    columns = projected.shape[1] // LANES
    for d in range(send_ref.shape[0]):
        h, j = divmod(d, columns)
        send_ref[d, :ROWS, :] = projected[
            h * ROWS : (h + 1) * ROWS, j * LANES : (j + 1) * LANES
        ]


def first_kernel(weighted_ref, field_ref, send_ref):
    store_tiles(send_ref, dot_wide(weighted_ref[...], field_ref[...], 0))


def reduce_kernel(side_ref, recv_ref, send_ref, *gram_ref, grp, pts):
    side = side_ref[0]
    for s in range(2):
        for c in range(grp):
            first = (s * grp + c) * pts
            total = recv_ref[first, :ROWS, :]
            for p in range(1, pts):
                total = total + recv_ref[first + p, :ROWS, :]
            for p in range(pts):
                send_ref[((1 - s) * grp + c) * pts + p] = total
    if gram_ref:
        first = (1 - side) * (grp * pts)
        total = recv_ref[first, ROWS:, :]
        for p in range(1, pts):
            total = total + recv_ref[first + p, ROWS:, :]
        gram_ref[0][...] = total


def factor_kernel(gram_ref, out_ref, *, modes, points):
    out_ref[...] = inverse_factor(unfold(gram_ref[...], modes) / points, modes)


def back_kernel(recv_ref, field_ref, out_ref):
    columns = field_ref.shape[1] // LANES
    count = recv_ref.shape[0] // columns
    coeffs = jnp.concatenate(
        [
            jnp.concatenate([recv_ref[h * columns + j] for j in range(columns)], axis=1)
            for h in range(count)
        ],
        axis=0,
    )
    out_ref[...] = dot_wide(coeffs, field_ref[...], 1)


def map_kernel(*refs, samples, others, has_factor, last):
    refs = list(refs)
    mapped = refs.pop(0)[...]
    modes, points = mapped.shape
    block = points // (others + 1)
    for k in range(others):
        other = refs.pop(0)[...]
        cut = (others - k) * block
        mapped = mapped + jnp.concatenate([other[:, cut:], other[:, :cut]], axis=1)
    factor = refs.pop(0)[...][:, :modes] if has_factor else None
    weight = refs.pop(0)[...]
    if has_factor:
        mapped = jnp.dot(factor, mapped, precision=HIGHEST, preferred_element_type=F32)
    mapped = mapped * weight if has_factor else mapped * weight / samples
    padded = jnp.concatenate([mapped, jnp.zeros((LANES - modes, points), F32)], axis=0)
    gram = lax.dot_general(
        mapped, padded, (((1,), (1,)), ((), ())), precision=HIGHEST, preferred_element_type=F32
    )
    tile = fold(gram, modes)
    if last:
        out_ref, send_ref = refs
        out_ref[...] = mapped[:, :block]
        for d in range(send_ref.shape[0]):
            send_ref[d] = tile
        return
    field_ref, send_ref = refs
    store_tiles(send_ref, dot_wide(mapped * weight, field_ref[...], 0))
    for d in range(send_ref.shape[0]):
        send_ref[d, ROWS:, :] = tile


def finish_kernel(side_ref, recv_ref, mapped_ref, out_ref, *, grp, pts, points):
    first = side_ref[0] * (grp * pts)
    total = recv_ref[first]
    for p in range(1, pts):
        total = total + recv_ref[first + p]
    mapped = mapped_ref[...]
    modes = mapped.shape[0]
    factor = inverse_factor(unfold(total, modes) / points, modes)[:, :modes]
    out_ref[...] = jnp.dot(factor, mapped, precision=HIGHEST, preferred_element_type=F32)


def call(kernel, outs, *args, cost=None):
    specs = [SMEM if a.dtype == jnp.int32 else VMEM for a in args]
    args = [
        a if a.dtype == jnp.int32 else pltpu.with_memory_space_constraint(a, pltpu.VMEM)
        for a in args
    ]
    many = isinstance(outs, list)
    return pl.pallas_call(
        kernel,
        out_shape=[pltpu.VMEM(o, F32) for o in outs] if many else pltpu.VMEM(outs, F32),
        in_specs=specs,
        out_specs=[VMEM for _ in outs] if many else VMEM,
        cost_estimate=cost,
    )(*args)


def exchange(value):
    return lax.all_to_all(value, ALL, 0, 0)


def shifted(value, shift):
    grp = lax.axis_size("grp")
    return lax.ppermute(value, "grp", [((i + shift) % grp, i) for i in range(grp)])


def body_tiles(fields, point_weight, start_modes):
    local_field, weight, modes0 = fields[0], point_weight, start_modes[0]
    modes, samples = modes0.shape[0], local_field.shape[1]
    grp, pts = lax.axis_size("grp"), lax.axis_size("pts")
    devices = 2 * grp * pts
    total_points = local_field.shape[0] * grp * pts
    columns = samples // grp
    place = lax.axis_index("grp")
    side = lax.axis_index("side").astype(jnp.int32).reshape(1)

    def part(member):
        return lax.dynamic_slice_in_dim(local_field, (member % grp) * columns, columns, 1)

    weighted = modes0 * weight
    blocks, weights, starts = [part(place)], [weight], [weighted]
    for k in range(1, grp):
        blocks.append(shifted(part(place - k), k))
        weights.append(shifted(weight, k))
        starts.append(shifted(weighted, k))
    field = jnp.concatenate(blocks, axis=0)
    weight = jnp.concatenate(weights, axis=1)
    start = jnp.concatenate(starts, axis=1)
    points = weight.shape[1]

    def reduced(recv, has_gram):
        shapes = [(devices, ROWS, LANES)] + [(ROWS, LANES)] * has_gram
        kernel = lambda *refs: reduce_kernel(*refs, grp=grp, pts=pts)
        return call(kernel, shapes, side, recv)

    factor = None
    send = call(first_kernel, (devices, ROWS, LANES), start, field)
    for iteration in range(ITERS):
        has_gram = iteration > 0
        out = reduced(exchange(send), has_gram)
        gathered = exchange(out[0])
        if has_gram:
            kernel = lambda *refs: factor_kernel(*refs, modes=modes, points=total_points)
            cost = pl.CostEstimate(flops=modes**3 << 10, bytes_accessed=ROWS * LANES * 4, transcendentals=0)
            factor = call(kernel, (modes, LANES), out[1], cost=cost) / samples
        own = call(back_kernel, (modes, points), gathered, field)
        others = [shifted(own, k) for k in range(1, grp)]
        last = iteration == ITERS - 1
        kernel = lambda *refs: map_kernel(
            *refs, samples=samples, others=grp - 1, has_factor=has_gram, last=last
        )
        given = [own, *others, *([factor] if has_gram else []), weight]
        if last:
            shapes = [(modes, points // grp), (devices, ROWS, LANES)]
            mapped, send = call(kernel, shapes, *given)
        else:
            send = call(kernel, (devices, 2 * ROWS, LANES), *given, field)
    kernel = lambda *refs: finish_kernel(*refs, grp=grp, pts=pts, points=total_points)
    return call(kernel, (modes, points // grp), side, exchange(send), mapped)[None]


def body_sums(fields, point_weight, start_modes):
    local_field, weight, mode_rows = fields[0], point_weight[0], start_modes[0]
    samples = local_field.shape[1]
    total_points = local_field.shape[0] * lax.axis_size("grp") * lax.axis_size("pts")
    for _ in range(ITERS):
        weighted = (mode_rows * weight[None, :]).astype(BF16)
        partial = jnp.dot(weighted, local_field, preferred_element_type=F32)
        coeffs = lax.psum(partial, ("grp", "pts")).astype(BF16)
        partner = lax.ppermute(coeffs, "side", [(0, 1), (1, 0)])
        mapped = lax.dot_general(
            partner, local_field, (((1,), (1,)), ((), ())), preferred_element_type=F32
        )
        mapped = mapped * weight[None, :] / samples
        gram = jnp.dot(mapped, mapped.T, precision=HIGHEST, preferred_element_type=F32)
        gram = lax.psum(gram, ("grp", "pts")) / total_points
        factor = jnp.linalg.cholesky(gram)
        mode_rows = lax.linalg.triangular_solve(factor, mapped, left_side=True, lower=True)
    return mode_rows[None]


def solution(mesh):
    grp, pts = mesh.shape["grp"], mesh.shape["pts"]

    def run(fields, point_weight, start_modes):
        modes, samples = start_modes.shape[1], fields.shape[2]
        tiles = (modes // ROWS) * (samples // (LANES * grp))
        fits = tiles == 2 * grp * pts and 4 * modes == LANES
        placed = (
            P("side", ("grp", "pts"), None),
            P("side", ("grp", "pts")),
            P("side", None, ("grp", "pts")),
        )
        return jax.shard_map(
            body_tiles if fits else body_sums,
            mesh=mesh,
            in_specs=placed,
            out_specs=P("side", None, ("grp", "pts")),
            check_vma=False,
        )(fields, point_weight, start_modes)

    return run
```

```python
import jax
import jax.numpy as jnp
from jax import lax
from jax.experimental import pallas as pl
from jax.experimental.pallas import tpu as pltpu
from jax.sharding import PartitionSpec as P

ITERS = 6
ROWS, LANES = 8, 128
ALL = ("side", "grp", "pts")
F32, BF16 = jnp.float32, jnp.bfloat16
HIGHEST = lax.Precision.HIGHEST
VMEM = pl.BlockSpec(memory_space=pltpu.VMEM)
SMEM = pl.BlockSpec(memory_space=pltpu.SMEM)


def split3(x):
    high = x.astype(BF16)
    rest = x - high.astype(F32)
    mid = rest.astype(BF16)
    low = (rest - mid.astype(F32)).astype(BF16)
    return jnp.concatenate([high, mid, low], axis=0)


def dot_wide(x, field, contract):
    count = x.shape[0]
    out = lax.dot_general(
        split3(x), field, (((1,), (contract,)), ((), ())), preferred_element_type=F32
    )
    return out[2 * count :] + out[count : 2 * count] + out[:count]


def fold(gram, modes):
    return sum(
        pltpu.roll(gram[g * ROWS : (g + 1) * ROWS], g * modes, 1) if g else gram[:ROWS]
        for g in range(modes // ROWS)
    )


def unfold(tile, modes):
    lane = lax.broadcasted_iota(jnp.int32, (ROWS, LANES), 1)
    parts = [
        pltpu.roll(tile, LANES - g * modes, 1) if g else tile for g in range(modes // ROWS)
    ]
    return jnp.concatenate([jnp.where(lane < modes, part, 0.0) for part in parts], axis=0)


def inverse_factor(gram, modes):
    row = lax.broadcasted_iota(jnp.int32, (modes, LANES), 0)
    lane = lax.broadcasted_iota(jnp.int32, (modes, LANES), 1)
    work = gram + jnp.where(lane == row + modes, 1.0, 0.0)
    for k in range(modes):
        top = work[k : k + 1]
        pivot = top[:, k : k + 1]
        factor = jnp.where(row > k, work[:, k : k + 1] / pivot, 0.0)
        work = work - factor * top
    pivots = jnp.sum(jnp.where(lane == row, work, 0.0), axis=1, keepdims=True)
    inverse = pltpu.roll(work, LANES - modes, 1) / jnp.sqrt(pivots)
    return jnp.where(lane < modes, inverse, 0.0)


def store_tiles(send_ref, projected):
    columns = projected.shape[1] // LANES
    for d in range(send_ref.shape[0]):
        h, j = divmod(d, columns)
        tile = projected[h * ROWS : (h + 1) * ROWS, j * LANES : (j + 1) * LANES]
        if send_ref.ndim == 3:
            send_ref[d] = tile
            continue
        slab = send_ref.shape[2]
        for k in range(ROWS // slab):
            send_ref[d, k] = tile[k * slab : (k + 1) * slab]


def own_slab(tile, place, grp):
    slab = ROWS // grp
    return sum(
        jnp.where(place == c, tile[c * slab : (c + 1) * slab], 0.0) for c in range(grp)
    )


def whole_tile(read, first, grp, pts):
    slabs = []
    for c in range(grp):
        total = read(first + c * pts)
        for p in range(1, pts):
            total = total + read(first + c * pts + p)
        slabs.append(total)
    return jnp.concatenate(slabs, axis=0)


def first_kernel(weighted_ref, field_ref, send_ref):
    store_tiles(send_ref, dot_wide(weighted_ref[...], field_ref[...], 0))


def reduce_kernel(side_ref, recv_ref, send_ref, *gram_ref, grp, pts):
    for s in range(2):
        for c in range(grp):
            first = (s * grp + c) * pts
            slabs = []
            for k in range(grp) if gram_ref else [...]:
                total = recv_ref[first, k]
                for p in range(1, pts):
                    total = total + recv_ref[first + p, k]
                slabs.append(total)
            total = jnp.concatenate(slabs, axis=0) if gram_ref else slabs[0]
            for p in range(pts):
                send_ref[((1 - s) * grp + c) * pts + p] = total
    if gram_ref:
        first = (1 - side_ref[0]) * (grp * pts)
        gram_ref[0][...] = whole_tile(lambda d: recv_ref[d, grp], first, grp, pts)


def factor_kernel(gram_ref, out_ref, *, modes, points):
    out_ref[...] = inverse_factor(unfold(gram_ref[...], modes) / points, modes)


def back_kernel(recv_ref, field_ref, out_ref):
    columns = field_ref.shape[1] // LANES
    count = recv_ref.shape[0] // columns
    coeffs = jnp.concatenate(
        [
            jnp.concatenate([recv_ref[h * columns + j] for j in range(columns)], axis=1)
            for h in range(count)
        ],
        axis=0,
    )
    out_ref[...] = dot_wide(coeffs, field_ref[...], 1)


def map_kernel(*refs, samples, others, has_factor, last):
    refs = list(refs)
    place, grp = refs.pop(0)[0], others + 1
    mapped = refs.pop(0)[...]
    modes, points = mapped.shape
    block = points // grp
    for k in range(others):
        other = refs.pop(0)[...]
        cut = (others - k) * block
        mapped = mapped + jnp.concatenate([other[:, cut:], other[:, :cut]], axis=1)
    factor = refs.pop(0)[...][:, :modes] if has_factor else None
    weight = refs.pop(0)[...]
    if has_factor:
        mapped = jnp.dot(factor, mapped, precision=HIGHEST, preferred_element_type=F32)
    mapped = mapped * weight if has_factor else mapped * weight / samples
    padded = jnp.concatenate([mapped, jnp.zeros((LANES - modes, points), F32)], axis=0)
    gram = lax.dot_general(
        mapped, padded, (((1,), (1,)), ((), ())), precision=HIGHEST, preferred_element_type=F32
    )
    slab = own_slab(fold(gram, modes), place, grp)
    if last:
        out_ref, send_ref = refs
        out_ref[...] = mapped[:, :block]
        for d in range(send_ref.shape[0]):
            send_ref[d] = slab
        return
    field_ref, send_ref = refs
    store_tiles(send_ref, dot_wide(mapped * weight, field_ref[...], 0))
    for d in range(send_ref.shape[0]):
        send_ref[d, grp] = slab


def finish_kernel(side_ref, recv_ref, mapped_ref, out_ref, *, grp, pts, points):
    total = whole_tile(lambda d: recv_ref[d], side_ref[0] * (grp * pts), grp, pts)
    mapped = mapped_ref[...]
    modes = mapped.shape[0]
    factor = inverse_factor(unfold(total, modes) / points, modes)[:, :modes]
    out_ref[...] = jnp.dot(factor, mapped, precision=HIGHEST, preferred_element_type=F32)


def call(kernel, outs, *args, cost=None):
    specs = [SMEM if a.dtype == jnp.int32 else VMEM for a in args]
    args = [
        a if a.dtype == jnp.int32 else pltpu.with_memory_space_constraint(a, pltpu.VMEM)
        for a in args
    ]
    many = isinstance(outs, list)
    return pl.pallas_call(
        kernel,
        out_shape=[pltpu.VMEM(o, F32) for o in outs] if many else pltpu.VMEM(outs, F32),
        in_specs=specs,
        out_specs=[VMEM for _ in outs] if many else VMEM,
        cost_estimate=cost,
    )(*args)


def exchange(value):
    return lax.all_to_all(value, ALL, 0, 0)


def shifted(value, shift):
    grp = lax.axis_size("grp")
    return lax.ppermute(value, "grp", [((i + shift) % grp, i) for i in range(grp)])


def body_tiles(fields, point_weight, start_modes):
    local_field, weight, modes0 = fields[0], point_weight, start_modes[0]
    modes, samples = modes0.shape[0], local_field.shape[1]
    grp, pts = lax.axis_size("grp"), lax.axis_size("pts")
    devices = 2 * grp * pts
    total_points = local_field.shape[0] * grp * pts
    columns = samples // grp
    place = lax.axis_index("grp").astype(jnp.int32).reshape(1)
    side = lax.axis_index("side").astype(jnp.int32).reshape(1)

    def part(member):
        member = member[0]
        return lax.dynamic_slice_in_dim(local_field, (member % grp) * columns, columns, 1)

    weighted = modes0 * weight
    blocks, weights, starts = [part(place)], [weight], [weighted]
    for k in range(1, grp):
        blocks.append(shifted(part(place - k), k))
        weights.append(shifted(weight, k))
        starts.append(shifted(weighted, k))
    field = jnp.concatenate(blocks, axis=0)
    weight = jnp.concatenate(weights, axis=1)
    start = jnp.concatenate(starts, axis=1)
    points = weight.shape[1]

    def reduced(recv, has_gram):
        shapes = [(devices, ROWS, LANES)] + [(ROWS, LANES)] * has_gram
        kernel = lambda *refs: reduce_kernel(*refs, grp=grp, pts=pts)
        return call(kernel, shapes, side, recv)

    factor = None
    send = call(first_kernel, (devices, ROWS, LANES), start, field)
    for iteration in range(ITERS):
        has_gram = iteration > 0
        out = reduced(exchange(send), has_gram)
        gathered = exchange(out[0])
        if has_gram:
            kernel = lambda *refs: factor_kernel(*refs, modes=modes, points=total_points)
            cost = pl.CostEstimate(flops=modes**3 << 10, bytes_accessed=ROWS * LANES * 4, transcendentals=0)
            factor = call(kernel, (modes, LANES), out[1], cost=cost) / samples
        own = call(back_kernel, (modes, points), gathered, field)
        others = [shifted(own, k) for k in range(1, grp)]
        last = iteration == ITERS - 1
        kernel = lambda *refs: map_kernel(
            *refs, samples=samples, others=grp - 1, has_factor=has_gram, last=last
        )
        given = [place, own, *others, *([factor] if has_gram else []), weight]
        if last:
            shapes = [(modes, points // grp), (devices, ROWS // grp, LANES)]
            mapped, send = call(kernel, shapes, *given)
        else:
            send = call(kernel, (devices, grp + 1, ROWS // grp, LANES), *given, field)
    kernel = lambda *refs: finish_kernel(*refs, grp=grp, pts=pts, points=total_points)
    return call(kernel, (modes, points // grp), side, exchange(send), mapped)[None]


def body_sums(fields, point_weight, start_modes):
    local_field, weight, mode_rows = fields[0], point_weight[0], start_modes[0]
    samples = local_field.shape[1]
    total_points = local_field.shape[0] * lax.axis_size("grp") * lax.axis_size("pts")
    for _ in range(ITERS):
        weighted = (mode_rows * weight[None, :]).astype(BF16)
        partial = jnp.dot(weighted, local_field, preferred_element_type=F32)
        coeffs = lax.psum(partial, ("grp", "pts")).astype(BF16)
        partner = lax.ppermute(coeffs, "side", [(0, 1), (1, 0)])
        mapped = lax.dot_general(
            partner, local_field, (((1,), (1,)), ((), ())), preferred_element_type=F32
        )
        mapped = mapped * weight[None, :] / samples
        gram = jnp.dot(mapped, mapped.T, precision=HIGHEST, preferred_element_type=F32)
        gram = lax.psum(gram, ("grp", "pts")) / total_points
        factor = jnp.linalg.cholesky(gram)
        mode_rows = lax.linalg.triangular_solve(factor, mapped, left_side=True, lower=True)
    return mode_rows[None]


def solution(mesh):
    grp, pts = mesh.shape["grp"], mesh.shape["pts"]

    def run(fields, point_weight, start_modes):
        modes, samples = start_modes.shape[1], fields.shape[2]
        tiles = (modes // ROWS) * (samples // (LANES * grp))
        fits = tiles == 2 * grp * pts and 4 * modes == LANES and ROWS % grp == 0
        placed = (
            P("side", ("grp", "pts"), None),
            P("side", ("grp", "pts")),
            P("side", None, ("grp", "pts")),
        )
        return jax.shard_map(
            body_tiles if fits else body_sums,
            mesh=mesh,
            in_specs=placed,
            out_specs=P("side", None, ("grp", "pts")),
            check_vma=False,
        )(fields, point_weight, start_modes)

    return run
```

```python
import jax
import jax.numpy as jnp
from jax import lax
from jax.experimental import pallas as pl
from jax.experimental.pallas import tpu as pltpu
from jax.sharding import PartitionSpec as P

ITERS = 6
ROWS, LANES = 8, 128
ALL = ("side", "grp", "pts")
F32, BF16 = jnp.float32, jnp.bfloat16
HIGHEST = lax.Precision.HIGHEST
VMEM = pl.BlockSpec(memory_space=pltpu.VMEM)
SMEM = pl.BlockSpec(memory_space=pltpu.SMEM)


def split3(x):
    high = x.astype(BF16)
    rest = x - high.astype(F32)
    mid = rest.astype(BF16)
    low = (rest - mid.astype(F32)).astype(BF16)
    return jnp.concatenate([high, mid, low], axis=0)


def dot_wide(x, field, contract):
    count = x.shape[0]
    out = lax.dot_general(
        split3(x), field, (((1,), (contract,)), ((), ())), preferred_element_type=F32
    )
    return out[2 * count :] + out[count : 2 * count] + out[:count]


def fold(gram, modes):
    return sum(
        pltpu.roll(gram[g * ROWS : (g + 1) * ROWS], g * modes, 1) if g else gram[:ROWS]
        for g in range(modes // ROWS)
    )


def unfold(tile, modes):
    lane = lax.broadcasted_iota(jnp.int32, (ROWS, LANES), 1)
    parts = [
        pltpu.roll(tile, LANES - g * modes, 1) if g else tile for g in range(modes // ROWS)
    ]
    return jnp.concatenate([jnp.where(lane < modes, part, 0.0) for part in parts], axis=0)


def inverse_factor(gram, modes):
    row = lax.broadcasted_iota(jnp.int32, (modes, LANES), 0)
    lane = lax.broadcasted_iota(jnp.int32, (modes, LANES), 1)
    work = gram + jnp.where(lane == row + modes, 1.0, 0.0)
    for k in range(0, modes, ROWS):
        rows = [work[k + j : k + j + 1] for j in range(ROWS)]
        columns = [
            jnp.broadcast_to(work[:, k + j : k + j + 1], (modes, LANES)) for j in range(ROWS)
        ]
        block = {
            (i, j): jnp.broadcast_to(rows[i][:, k + j : k + j + 1], (1, LANES))
            for i in range(ROWS)
            for j in range(i, ROWS)
        }
        factors = []
        for j in range(ROWS):
            inverse = 1.0 / block[j, j]
            factor = jnp.where(row > k + j, columns[j] * inverse, 0.0)
            factors.append(factor)
            for i in range(j + 1, ROWS):
                columns[i] = columns[i] - factor * block[j, i]
                ratio = block[j, i] * inverse
                for c in range(i, ROWS):
                    block[i, c] = block[i, c] - ratio * block[j, c]
                rows[i] = rows[i] - ratio * rows[j]
        for j in range(ROWS):
            work = work - factors[j] * rows[j]
    pivots = jnp.sum(jnp.where(lane == row, work, 0.0), axis=1, keepdims=True)
    inverse = pltpu.roll(work, LANES - modes, 1) / jnp.sqrt(pivots)
    return jnp.where(lane < modes, inverse, 0.0)


def store_tiles(send_ref, projected):
    columns = projected.shape[1] // LANES
    for d in range(send_ref.shape[0]):
        h, j = divmod(d, columns)
        tile = projected[h * ROWS : (h + 1) * ROWS, j * LANES : (j + 1) * LANES]
        if send_ref.ndim == 3:
            send_ref[d] = tile
            continue
        slab = send_ref.shape[2]
        for k in range(ROWS // slab):
            send_ref[d, k] = tile[k * slab : (k + 1) * slab]


def own_slab(tile, place, grp):
    slab = ROWS // grp
    return sum(
        jnp.where(place == c, tile[c * slab : (c + 1) * slab], 0.0) for c in range(grp)
    )


def whole_tile(read, first, grp, pts):
    slabs = []
    for c in range(grp):
        total = read(first + c * pts)
        for p in range(1, pts):
            total = total + read(first + c * pts + p)
        slabs.append(total)
    return jnp.concatenate(slabs, axis=0)


def setup_kernel(place_ref, fields_ref, weight_ref, modes_ref, pack_ref, *rest):
    *block_refs, sems = rest
    grp, columns = len(block_refs), block_refs[0].shape[1]
    copies = []
    for k in reversed(range(grp)):
        start = pl.multiple_of(lax.rem(place_ref[0] + grp - k, grp) * columns, LANES)
        copies.append(
            pltpu.make_async_copy(
                fields_ref.at[0, :, pl.ds(start, columns)], block_refs[k], sems.at[k]
            )
        )
        copies[-1].start()
    modes = modes_ref.shape[1]
    pack_ref[:modes] = modes_ref[0]
    pack_ref[modes:] = jnp.broadcast_to(weight_ref[...], (ROWS, weight_ref.shape[1]))
    for copy in copies:
        copy.wait()


def first_kernel(*refs):
    *pack_refs, field_ref, send_ref, weight_ref = refs
    pack = jnp.concatenate([ref[...] for ref in pack_refs], axis=1)
    weight = pack[-ROWS:]
    weight_ref[...] = weight
    store_tiles(send_ref, dot_wide(pack[:-ROWS] * weight[:1], field_ref[...], 0))


def reduce_kernel(side_ref, recv_ref, send_ref, *gram_ref, grp, pts):
    for s in range(2):
        for c in range(grp):
            first = (s * grp + c) * pts
            slabs = []
            for k in range(grp) if gram_ref else [...]:
                total = recv_ref[first, k]
                for p in range(1, pts):
                    total = total + recv_ref[first + p, k]
                slabs.append(total)
            total = jnp.concatenate(slabs, axis=0) if gram_ref else slabs[0]
            for p in range(pts):
                send_ref[((1 - s) * grp + c) * pts + p] = total.astype(send_ref.dtype)
    if gram_ref:
        first = (1 - side_ref[0]) * (grp * pts)
        gram_ref[0][...] = whole_tile(lambda d: recv_ref[d, grp], first, grp, pts)


def factor_kernel(gram_ref, out_ref, *, modes, points):
    out_ref[...] = inverse_factor(unfold(gram_ref[...], modes) / points, modes)


def back_kernel(recv_ref, field_ref, out_ref):
    columns = field_ref.shape[1] // LANES
    count = recv_ref.shape[0] // columns
    coeffs = jnp.concatenate(
        [
            jnp.concatenate([recv_ref[h * columns + j] for j in range(columns)], axis=1)
            for h in range(count)
        ],
        axis=0,
    )
    if coeffs.dtype == BF16:
        out_ref[...] = lax.dot_general(
            coeffs, field_ref[...], (((1,), (1,)), ((), ())), preferred_element_type=F32
        )
    else:
        out_ref[...] = dot_wide(coeffs, field_ref[...], 1)


def map_kernel(*refs, samples, others, has_factor, last):
    refs = list(refs)
    place, grp = refs.pop(0)[0], others + 1
    mapped = refs.pop(0)[...]
    modes, points = mapped.shape
    block = points // grp
    for k in range(others):
        other = refs.pop(0)[...]
        cut = (others - k) * block
        mapped = mapped + jnp.concatenate([other[:, cut:], other[:, :cut]], axis=1)
    factor = refs.pop(0)[...][:, :modes] if has_factor else None
    weight = refs.pop(0)[:1]
    if has_factor:
        mapped = jnp.dot(factor, mapped, precision=HIGHEST, preferred_element_type=F32)
    mapped = mapped * weight / samples
    padded = jnp.concatenate([mapped, jnp.zeros((LANES - modes, points), F32)], axis=0)
    gram = lax.dot_general(
        mapped, padded, (((1,), (1,)), ((), ())), precision=HIGHEST, preferred_element_type=F32
    )
    slab = own_slab(fold(gram, modes), place, grp)
    if last:
        out_ref, send_ref = refs
        out_ref[...] = mapped[:, :block]
        for d in range(send_ref.shape[0]):
            send_ref[d] = slab
        return
    field_ref, send_ref = refs
    store_tiles(send_ref, dot_wide(mapped * weight, field_ref[...], 0))
    for d in range(send_ref.shape[0]):
        send_ref[d, grp] = slab


def finish_kernel(side_ref, recv_ref, mapped_ref, out_ref, *, grp, pts, points):
    total = whole_tile(lambda d: recv_ref[d], side_ref[0] * (grp * pts), grp, pts)
    mapped = mapped_ref[...]
    modes = mapped.shape[0]
    factor = inverse_factor(unfold(total, modes) / points, modes)[:, :modes]
    out_ref[...] = jnp.dot(factor, mapped, precision=HIGHEST, preferred_element_type=F32)


def call(kernel, outs, *args):
    specs = [SMEM if a.dtype == jnp.int32 else VMEM for a in args]
    args = [
        a if a.dtype == jnp.int32 else pltpu.with_memory_space_constraint(a, pltpu.VMEM)
        for a in args
    ]
    out = [o if isinstance(o, jax.ShapeDtypeStruct) else pltpu.VMEM(*o) for o in outs]
    result = pl.pallas_call(
        kernel, out_shape=out, in_specs=specs, out_specs=[VMEM for _ in out]
    )(*args)
    return result if len(out) > 1 else result[0]


def cut(place, fields, weight, modes, grp):
    _, points, samples = fields.shape
    out = [pltpu.VMEM((modes.shape[1] + ROWS, points), F32)]
    out += [pltpu.VMEM((points, samples // grp), fields.dtype) for _ in range(grp)]
    anywhere = pl.BlockSpec(memory_space=pl.ANY)
    return pl.pallas_call(
        setup_kernel,
        out_shape=out,
        in_specs=[SMEM, anywhere, VMEM, VMEM],
        out_specs=[VMEM for _ in out],
        scratch_shapes=[pltpu.SemaphoreType.DMA((grp,))],
    )(place, fields, weight, modes)


def exchange(value):
    return lax.all_to_all(value, ALL, 0, 0)


def shifted(value, shift):
    grp = lax.axis_size("grp")
    return lax.ppermute(value, "grp", [((i + shift) % grp, i) for i in range(grp)])


def body_tiles(fields, point_weight, start_modes):
    modes, samples = start_modes.shape[1], fields.shape[2]
    grp, pts = lax.axis_size("grp"), lax.axis_size("pts")
    devices = 2 * grp * pts
    total_points = fields.shape[1] * grp * pts
    points = fields.shape[1] * grp
    place = lax.axis_index("grp").astype(jnp.int32).reshape(1)
    side = lax.axis_index("side").astype(jnp.int32).reshape(1)

    pack, *blocks = cut(place, fields, point_weight, start_modes, grp)
    packs = [pack] + [shifted(pack, k) for k in range(1, grp)]
    field = jnp.concatenate(
        [blocks[0]] + [shifted(blocks[k], k) for k in range(1, grp)], axis=0
    )
    tile = (devices, ROWS, LANES)
    slabs = (devices, grp + 1, ROWS // grp, LANES)

    factor = None
    send, weight = call(first_kernel, [(tile, F32), ((ROWS, points), F32)], *packs, field)
    for iteration in range(ITERS):
        has_gram, last = iteration > 0, iteration == ITERS - 1
        kernel = lambda *refs: reduce_kernel(*refs, grp=grp, pts=pts)
        if has_gram:
            outs = [(tile, F32), ((ROWS, LANES), F32)]
            summed, gram = call(kernel, outs, side, exchange(send))
        else:
            summed = call(kernel, [(tile, BF16)], side, exchange(send))
        own = call(back_kernel, [((modes, points), F32)], exchange(summed), field)
        others = [shifted(own, k) for k in range(1, grp)]
        if has_gram:
            kernel = lambda *refs: factor_kernel(*refs, modes=modes, points=total_points)
            factor = call(kernel, [((modes, LANES), F32)], gram)
        kernel = lambda *refs: map_kernel(
            *refs, samples=samples, others=grp - 1, has_factor=has_gram, last=last
        )
        given = [place, own, *others, *([factor] if has_gram else []), weight]
        if last:
            outs = [((modes, points // grp), F32), ((devices, ROWS // grp, LANES), F32)]
            mapped, send = call(kernel, outs, *given)
        else:
            send = call(kernel, [(slabs, F32)], *given, field)
    kernel = lambda *refs: finish_kernel(*refs, grp=grp, pts=pts, points=total_points)
    out = jax.ShapeDtypeStruct((modes, points // grp), F32)
    return call(kernel, [out], side, exchange(send), mapped)[None]


def body_sums(fields, point_weight, start_modes):
    local_field, weight, mode_rows = fields[0], point_weight[0], start_modes[0]
    samples = local_field.shape[1]
    total_points = local_field.shape[0] * lax.axis_size("grp") * lax.axis_size("pts")
    for _ in range(ITERS):
        weighted = (mode_rows * weight[None, :]).astype(BF16)
        partial = jnp.dot(weighted, local_field, preferred_element_type=F32)
        coeffs = lax.psum(partial, ("grp", "pts")).astype(BF16)
        partner = lax.ppermute(coeffs, "side", [(0, 1), (1, 0)])
        mapped = lax.dot_general(
            partner, local_field, (((1,), (1,)), ((), ())), preferred_element_type=F32
        )
        mapped = mapped * weight[None, :] / samples
        gram = jnp.dot(mapped, mapped.T, precision=HIGHEST, preferred_element_type=F32)
        gram = lax.psum(gram, ("grp", "pts")) / total_points
        factor = jnp.linalg.cholesky(gram)
        mode_rows = lax.linalg.triangular_solve(factor, mapped, left_side=True, lower=True)
    return mode_rows[None]


def solution(mesh):
    grp, pts = mesh.shape["grp"], mesh.shape["pts"]

    def run(fields, point_weight, start_modes):
        modes, samples = start_modes.shape[1], fields.shape[2]
        tiles = (modes // ROWS) * (samples // (LANES * grp))
        fits = tiles == 2 * grp * pts and 4 * modes == LANES and ROWS % grp == 0
        placed = (
            P("side", ("grp", "pts"), None),
            P("side", ("grp", "pts")),
            P("side", None, ("grp", "pts")),
        )
        return jax.shard_map(
            body_tiles if fits else body_sums,
            mesh=mesh,
            in_specs=placed,
            out_specs=P("side", None, ("grp", "pts")),
            check_vma=False,
        )(fields, point_weight, start_modes)

    return run
```

```python
import jax
import jax.numpy as jnp
from jax import lax
from jax.experimental import pallas as pl
from jax.experimental.pallas import tpu as pltpu
from jax.sharding import PartitionSpec as P

ITERS = 6
ROWS, LANES = 8, 128
ALL = ("side", "grp", "pts")
F32, BF16 = jnp.float32, jnp.bfloat16
HIGHEST = lax.Precision.HIGHEST
VMEM = pl.BlockSpec(memory_space=pltpu.VMEM)
SMEM = pl.BlockSpec(memory_space=pltpu.SMEM)


def split3(x):
    high = x.astype(BF16)
    rest = x - high.astype(F32)
    mid = rest.astype(BF16)
    low = (rest - mid.astype(F32)).astype(BF16)
    return jnp.concatenate([high, mid, low], axis=0)


def dot_wide(x, field, contract):
    count = x.shape[0]
    out = lax.dot_general(
        split3(x), field, (((1,), (contract,)), ((), ())), preferred_element_type=F32
    )
    return out[2 * count :] + out[count : 2 * count] + out[:count]


def fold(gram, modes):
    return sum(
        pltpu.roll(gram[g * ROWS : (g + 1) * ROWS], g * modes, 1) if g else gram[:ROWS]
        for g in range(modes // ROWS)
    )


def unfold(tile, modes):
    lane = lax.broadcasted_iota(jnp.int32, (ROWS, LANES), 1)
    parts = [
        pltpu.roll(tile, LANES - g * modes, 1) if g else tile for g in range(modes // ROWS)
    ]
    return jnp.concatenate([jnp.where(lane < modes, part, 0.0) for part in parts], axis=0)


def inverse_factor(gram, modes):
    row = lax.broadcasted_iota(jnp.int32, (modes, LANES), 0)
    lane = lax.broadcasted_iota(jnp.int32, (modes, LANES), 1)
    work = gram + jnp.where(lane == row + modes, 1.0, 0.0)
    for k in range(0, modes, ROWS):
        rows = [work[k + j : k + j + 1] for j in range(ROWS)]
        columns = [
            jnp.broadcast_to(work[:, k + j : k + j + 1], (modes, LANES)) for j in range(ROWS)
        ]
        block = {
            (i, j): jnp.broadcast_to(rows[i][:, k + j : k + j + 1], (1, LANES))
            for i in range(ROWS)
            for j in range(i, ROWS)
        }
        factors = []
        for j in range(ROWS):
            inverse = 1.0 / block[j, j]
            factor = jnp.where(row > k + j, columns[j] * inverse, 0.0)
            factors.append(factor)
            for i in range(j + 1, ROWS):
                columns[i] = columns[i] - factor * block[j, i]
                ratio = block[j, i] * inverse
                for c in range(i, ROWS):
                    block[i, c] = block[i, c] - ratio * block[j, c]
                rows[i] = rows[i] - ratio * rows[j]
        for j in range(ROWS):
            work = work - factors[j] * rows[j]
    pivots = jnp.sum(jnp.where(lane == row, work, 0.0), axis=1, keepdims=True)
    inverse = pltpu.roll(work, LANES - modes, 1) / jnp.sqrt(pivots)
    return jnp.where(lane < modes, inverse, 0.0)


def store_tiles(send_ref, projected, pitch):
    columns = projected.shape[1] // LANES
    for d in range(send_ref.shape[0] // pitch):
        h, j = divmod(d, columns)
        send_ref[d * pitch : d * pitch + ROWS] = projected[
            h * ROWS : (h + 1) * ROWS, j * LANES : (j + 1) * LANES
        ]


def own_slab(tile, place, grp):
    slab = ROWS // grp
    return sum(
        jnp.where(place == c, tile[c * slab : (c + 1) * slab], 0.0) for c in range(grp)
    )


def whole_tile(read, first, grp, pts):
    slabs = []
    for c in range(grp):
        total = read(first + c * pts)
        for p in range(1, pts):
            total = total + read(first + c * pts + p)
        slabs.append(total)
    return jnp.concatenate(slabs, axis=0)


def setup_kernel(place_ref, fields_ref, weight_ref, modes_ref, pack_ref, *rest):
    *block_refs, row_ref, sems = rest
    grp, columns = len(block_refs), block_refs[0].shape[1]
    modes = modes_ref.shape[1]
    pairs = [(weight_ref, row_ref), (modes_ref.at[0], pack_ref.at[:modes])]
    for k in reversed(range(grp)):
        start = pl.multiple_of(lax.rem(place_ref[0] + grp - k, grp) * columns, LANES)
        pairs.append((fields_ref.at[0, :, pl.ds(start, columns)], block_refs[k]))
    copies = [
        pltpu.make_async_copy(source, target, sems.at[i])
        for i, (source, target) in enumerate(pairs)
    ]
    for copy in copies:
        copy.start()
    copies[0].wait()
    pack_ref[modes:] = jnp.broadcast_to(row_ref[...], (ROWS, row_ref.shape[1]))
    for copy in copies[1:]:
        copy.wait()


def first_kernel(*refs):
    *pack_refs, field_ref, send_ref, weight_ref = refs
    pack = jnp.concatenate([ref[...] for ref in pack_refs], axis=1)
    weight = pack[-ROWS:]
    weight_ref[...] = weight
    store_tiles(send_ref, dot_wide(pack[:-ROWS] * weight[:1], field_ref[...], 0), ROWS)


def reduce_kernel(recv_ref, send_ref, *, grp, pts, pitch):
    def total(first, rows):
        parts = [recv_ref[d * pitch + rows.start : d * pitch + rows.stop] for d in
                 range(first, first + pts)]
        return sum(parts[1:], parts[0])

    for s in range(2):
        gram = total(s * grp * pts, slice(ROWS, pitch)) if pitch > ROWS else None
        for c in range(grp):
            tile = total((s * grp + c) * pts, slice(0, ROWS)).astype(send_ref.dtype)
            for p in range(pts):
                first = (((1 - s) * grp + c) * pts + p) * pitch
                send_ref[first : first + ROWS] = tile
                if pitch > ROWS:
                    send_ref[first + ROWS : first + pitch] = gram


def factor_kernel(recv_ref, out_ref, *, modes, points, pitch):
    gram = jnp.concatenate(
        [recv_ref[r * pitch + ROWS : (r + 1) * pitch] for r in range(ROWS)], axis=0
    )
    out_ref[...] = inverse_factor(unfold(gram, modes) / points, modes)


def back_kernel(recv_ref, field_ref, out_ref, *, pitch):
    columns = field_ref.shape[1] // LANES
    count = recv_ref.shape[0] // (pitch * columns)
    coeffs = jnp.concatenate(
        [
            jnp.concatenate(
                [
                    recv_ref[(h * columns + j) * pitch : (h * columns + j) * pitch + ROWS]
                    for j in range(columns)
                ],
                axis=1,
            )
            for h in range(count)
        ],
        axis=0,
    )
    if coeffs.dtype == BF16:
        out_ref[...] = lax.dot_general(
            coeffs, field_ref[...], (((1,), (1,)), ((), ())), preferred_element_type=F32
        )
    else:
        out_ref[...] = dot_wide(coeffs, field_ref[...], 1)


def map_kernel(*refs, samples, others, has_factor, last):
    refs = list(refs)
    place, grp = refs.pop(0)[0], others + 1
    mapped = refs.pop(0)[...]
    modes, points = mapped.shape
    block = points // grp
    for k in range(others):
        other = refs.pop(0)[...]
        cut = (others - k) * block
        mapped = mapped + jnp.concatenate([other[:, cut:], other[:, :cut]], axis=1)
    factor = refs.pop(0)[...][:, :modes] if has_factor else None
    weight = refs.pop(0)[:1]
    if has_factor:
        mapped = jnp.dot(factor, mapped, precision=HIGHEST, preferred_element_type=F32)
    mapped = mapped * weight / samples
    padded = jnp.concatenate([mapped, jnp.zeros((LANES - modes, points), F32)], axis=0)
    gram = lax.dot_general(
        mapped, padded, (((1,), (1,)), ((), ())), precision=HIGHEST, preferred_element_type=F32
    )
    tile = fold(gram, modes)
    if last:
        out_ref, send_ref = refs
        out_ref[...] = mapped[:, :block]
        slab = own_slab(tile, place, grp)
        for d in range(send_ref.shape[0]):
            send_ref[d] = slab
        return
    field_ref, send_ref = refs
    pitch = ROWS + 1
    store_tiles(send_ref, dot_wide(mapped * weight, field_ref[...], 0), pitch)
    for d in range(send_ref.shape[0] // pitch):
        send_ref[d * pitch + ROWS : (d + 1) * pitch] = tile[d % ROWS : d % ROWS + 1]


def finish_kernel(side_ref, recv_ref, mapped_ref, out_ref, *, grp, pts, points):
    total = whole_tile(lambda d: recv_ref[d], side_ref[0] * (grp * pts), grp, pts)
    mapped = mapped_ref[...]
    modes = mapped.shape[0]
    factor = inverse_factor(unfold(total, modes) / points, modes)[:, :modes]
    out_ref[...] = jnp.dot(factor, mapped, precision=HIGHEST, preferred_element_type=F32)


def call(kernel, outs, *args):
    specs = [SMEM if a.dtype == jnp.int32 else VMEM for a in args]
    args = [
        a if a.dtype == jnp.int32 else pltpu.with_memory_space_constraint(a, pltpu.VMEM)
        for a in args
    ]
    out = [o if isinstance(o, jax.ShapeDtypeStruct) else pltpu.VMEM(*o) for o in outs]
    result = pl.pallas_call(
        kernel, out_shape=out, in_specs=specs, out_specs=[VMEM for _ in out]
    )(*args)
    return result if len(out) > 1 else result[0]


def cut(place, fields, weight, modes, grp):
    _, points, samples = fields.shape
    out = [pltpu.VMEM((modes.shape[1] + ROWS, points), F32)]
    out += [pltpu.VMEM((points, samples // grp), fields.dtype) for _ in range(grp)]
    anywhere = pl.BlockSpec(memory_space=pl.ANY)
    return pl.pallas_call(
        setup_kernel,
        out_shape=out,
        in_specs=[SMEM, anywhere, anywhere, anywhere],
        out_specs=[VMEM for _ in out],
        scratch_shapes=[pltpu.VMEM((1, points), F32), pltpu.SemaphoreType.DMA((grp + 2,))],
    )(place, fields, weight, modes)


def exchange(value, pitch=None):
    if pitch is None:
        return lax.all_to_all(value, ALL, 0, 0)
    chunks = value.shape[0] // pitch
    unit = ROWS if pitch == ROWS else 1
    split = value.reshape(chunks, pitch // unit, unit, LANES)
    return lax.all_to_all(split, ALL, 0, 0).reshape(value.shape)


def shifted(value, shift):
    grp = lax.axis_size("grp")
    return lax.ppermute(value, "grp", [((i + shift) % grp, i) for i in range(grp)])


def body_tiles(fields, point_weight, start_modes):
    modes, samples = start_modes.shape[1], fields.shape[2]
    grp, pts = lax.axis_size("grp"), lax.axis_size("pts")
    devices = 2 * grp * pts
    total_points = fields.shape[1] * grp * pts
    points = fields.shape[1] * grp
    place = lax.axis_index("grp").astype(jnp.int32).reshape(1)
    side = lax.axis_index("side").astype(jnp.int32).reshape(1)

    pack, *blocks = cut(place, fields, point_weight, start_modes, grp)
    packs = [pack] + [shifted(pack, k) for k in range(1, grp)]
    field = jnp.concatenate(
        [blocks[0]] + [shifted(blocks[k], k) for k in range(1, grp)], axis=0
    )
    factor, pitch = None, ROWS
    outs = [((devices * ROWS, LANES), F32), ((ROWS, points), F32)]
    send, weight = call(first_kernel, outs, *packs, field)
    for iteration in range(ITERS):
        has_gram, last = iteration > 0, iteration == ITERS - 1
        kernel = lambda *refs: reduce_kernel(*refs, grp=grp, pts=pts, pitch=pitch)
        dtype = F32 if has_gram else BF16
        summed = call(kernel, [((devices * pitch, LANES), dtype)], exchange(send, pitch))
        gathered = exchange(summed, pitch)
        kernel = lambda *refs: back_kernel(*refs, pitch=pitch)
        own = call(kernel, [((modes, points), F32)], gathered, field)
        others = [shifted(own, k) for k in range(1, grp)]
        if has_gram:
            kernel = lambda *refs: factor_kernel(
                *refs, modes=modes, points=total_points, pitch=pitch
            )
            factor = call(kernel, [((modes, LANES), F32)], gathered)
        pitch = ROWS + 1
        kernel = lambda *refs: map_kernel(
            *refs, samples=samples, others=grp - 1, has_factor=has_gram, last=last
        )
        given = [place, own, *others, *([factor] if has_gram else []), weight]
        if last:
            outs = [((modes, points // grp), F32), ((devices, ROWS // grp, LANES), F32)]
            mapped, send = call(kernel, outs, *given)
        else:
            send = call(kernel, [((devices * pitch, LANES), F32)], *given, field)
    kernel = lambda *refs: finish_kernel(*refs, grp=grp, pts=pts, points=total_points)
    out = jax.ShapeDtypeStruct((modes, points // grp), F32)
    return call(kernel, [out], side, exchange(send), mapped)[None]


def body_sums(fields, point_weight, start_modes):
    local_field, weight, mode_rows = fields[0], point_weight[0], start_modes[0]
    samples = local_field.shape[1]
    total_points = local_field.shape[0] * lax.axis_size("grp") * lax.axis_size("pts")
    for _ in range(ITERS):
        weighted = (mode_rows * weight[None, :]).astype(BF16)
        partial = jnp.dot(weighted, local_field, preferred_element_type=F32)
        coeffs = lax.psum(partial, ("grp", "pts")).astype(BF16)
        partner = lax.ppermute(coeffs, "side", [(0, 1), (1, 0)])
        mapped = lax.dot_general(
            partner, local_field, (((1,), (1,)), ((), ())), preferred_element_type=F32
        )
        mapped = mapped * weight[None, :] / samples
        gram = jnp.dot(mapped, mapped.T, precision=HIGHEST, preferred_element_type=F32)
        gram = lax.psum(gram, ("grp", "pts")) / total_points
        factor = jnp.linalg.cholesky(gram)
        mode_rows = lax.linalg.triangular_solve(factor, mapped, left_side=True, lower=True)
    return mode_rows[None]


def solution(mesh):
    grp, pts = mesh.shape["grp"], mesh.shape["pts"]

    def run(fields, point_weight, start_modes):
        modes, samples = start_modes.shape[1], fields.shape[2]
        tiles = (modes // ROWS) * (samples // (LANES * grp))
        fits = tiles == 2 * grp * pts and 4 * modes == LANES and ROWS % grp == 0
        placed = (
            P("side", ("grp", "pts"), None),
            P("side", ("grp", "pts")),
            P("side", None, ("grp", "pts")),
        )
        return jax.shard_map(
            body_tiles if fits else body_sums,
            mesh=mesh,
            in_specs=placed,
            out_specs=P("side", None, ("grp", "pts")),
            check_vma=False,
        )(fields, point_weight, start_modes)

    return run
```

```python
import jax
import jax.numpy as jnp
from jax import lax
from jax.experimental import pallas as pl
from jax.experimental.pallas import tpu as pltpu
from jax.sharding import PartitionSpec as P

ITERS = 6
ROWS, LANES = 8, 128
ALL = ("side", "grp", "pts")
F32, BF16 = jnp.float32, jnp.bfloat16
HIGHEST = lax.Precision.HIGHEST
VMEM = pl.BlockSpec(memory_space=pltpu.VMEM)
SMEM = pl.BlockSpec(memory_space=pltpu.SMEM)


def split3(x):
    high = x.astype(BF16)
    rest = x - high.astype(F32)
    mid = rest.astype(BF16)
    low = (rest - mid.astype(F32)).astype(BF16)
    return jnp.concatenate([high, mid, low], axis=0)


def dot_wide(x, field):
    count = x.shape[0]
    out = jnp.dot(split3(x), field, preferred_element_type=F32)
    return out[2 * count :] + out[count : 2 * count] + out[:count]


def fold(gram, modes):
    return sum(
        pltpu.roll(gram[g * ROWS : (g + 1) * ROWS], g * modes, 1) if g else gram[:ROWS]
        for g in range(modes // ROWS)
    )


def unfold(tile, modes):
    lane = lax.broadcasted_iota(jnp.int32, (ROWS, LANES), 1)
    parts = [
        pltpu.roll(tile, LANES - g * modes, 1) if g else tile for g in range(modes // ROWS)
    ]
    return jnp.concatenate([jnp.where(lane < modes, part, 0.0) for part in parts], axis=0)


def inverse_factor(gram, modes):
    row = lax.broadcasted_iota(jnp.int32, (modes, LANES), 0)
    lane = lax.broadcasted_iota(jnp.int32, (modes, LANES), 1)
    work = gram + jnp.where(lane == row + modes, 1.0, 0.0)
    for k in range(0, modes, ROWS):
        rows = [work[k + j : k + j + 1] for j in range(ROWS)]
        columns = [
            jnp.broadcast_to(work[:, k + j : k + j + 1], (modes, LANES)) for j in range(ROWS)
        ]
        block = {
            (i, j): jnp.broadcast_to(rows[i][:, k + j : k + j + 1], (1, LANES))
            for i in range(ROWS)
            for j in range(i, ROWS)
        }
        factors = []
        for j in range(ROWS):
            inverse = 1.0 / block[j, j]
            factor = jnp.where(row > k + j, columns[j] * inverse, 0.0)
            factors.append(factor)
            for i in range(j + 1, ROWS):
                columns[i] = columns[i] - factor * block[j, i]
                ratio = block[j, i] * inverse
                for c in range(i, ROWS):
                    block[i, c] = block[i, c] - ratio * block[j, c]
                rows[i] = rows[i] - ratio * rows[j]
        for j in range(ROWS):
            work = work - factors[j] * rows[j]
    pivots = jnp.sum(jnp.where(lane == row, work, 0.0), axis=1, keepdims=True)
    inverse = pltpu.roll(work, LANES - modes, 1) / jnp.sqrt(pivots)
    return jnp.where(lane < modes, inverse, 0.0)


def store_tiles(send_ref, projected, pitch):
    columns = projected.shape[1] // LANES
    for d in range(send_ref.shape[0] // pitch):
        h, j = divmod(d, columns)
        send_ref[d * pitch : d * pitch + ROWS] = projected[
            h * ROWS : (h + 1) * ROWS, j * LANES : (j + 1) * LANES
        ]


def own_slab(tile, place, grp):
    slab = ROWS // grp
    return sum(
        jnp.where(place == c, tile[c * slab : (c + 1) * slab], 0.0) for c in range(grp)
    )


def whole_tile(read, first, grp, pts):
    slabs = []
    for c in range(grp):
        total = read(first + c * pts)
        for p in range(1, pts):
            total = total + read(first + c * pts + p)
        slabs.append(total)
    return jnp.concatenate(slabs, axis=0)


def setup_kernel(place_ref, fields_ref, weight_ref, modes_ref, pack_ref, *rest):
    *block_refs, row_ref, sems = rest
    grp, columns = len(block_refs), block_refs[0].shape[1]
    modes = modes_ref.shape[1]
    pairs = [(weight_ref, row_ref), (modes_ref.at[0], pack_ref.at[:modes])]
    for k in reversed(range(grp)):
        start = pl.multiple_of(lax.rem(place_ref[0] + grp - k, grp) * columns, LANES)
        pairs.append((fields_ref.at[0, :, pl.ds(start, columns)], block_refs[k]))
    copies = [
        pltpu.make_async_copy(source, target, sems.at[i])
        for i, (source, target) in enumerate(pairs)
    ]
    for copy in copies:
        copy.start()
    copies[0].wait()
    pack_ref[modes:] = jnp.broadcast_to(row_ref[...], (ROWS, row_ref.shape[1]))
    for copy in copies[1:]:
        copy.wait()


def first_kernel(*refs):
    *pack_refs, field_ref, send_ref, weight_ref = refs
    pack = jnp.concatenate([ref[...] for ref in pack_refs], axis=1)
    weight = pack[-ROWS:]
    weight_ref[...] = weight
    store_tiles(send_ref, dot_wide(pack[:-ROWS] * weight[:1], field_ref[...]), ROWS)


def reduce_kernel(recv_ref, send_ref, *, grp, pts, pitch):
    def total(first, rows):
        parts = [recv_ref[d * pitch + rows.start : d * pitch + rows.stop] for d in
                 range(first, first + pts)]
        return sum(parts[1:], parts[0])

    for s in range(2):
        gram = total(s * grp * pts, slice(ROWS, pitch)) if pitch > ROWS else None
        for c in range(grp):
            tile = total((s * grp + c) * pts, slice(0, ROWS)).astype(send_ref.dtype)
            for p in range(pts):
                first = (((1 - s) * grp + c) * pts + p) * pitch
                send_ref[first : first + ROWS] = tile
                if pitch > ROWS:
                    send_ref[first + ROWS : first + pitch] = gram


def factor_kernel(recv_ref, out_ref, *, modes, points, pitch):
    gram = jnp.concatenate(
        [recv_ref[r * pitch + ROWS : (r + 1) * pitch] for r in range(ROWS)], axis=0
    )
    out_ref[...] = inverse_factor(unfold(gram, modes) / points, modes)


def back_kernel(recv_ref, field_ref, out_ref, *, pitch, samples):
    columns = samples // LANES
    count = recv_ref.shape[0] // (pitch * columns)
    coeffs = jnp.concatenate(
        [
            jnp.concatenate(
                [
                    recv_ref[(h * columns + j) * pitch : (h * columns + j) * pitch + ROWS]
                    for j in range(columns)
                ],
                axis=1,
            )
            for h in range(count)
        ],
        axis=0,
    )
    if coeffs.dtype == BF16:
        out_ref[...] = lax.dot_general(
            coeffs, field_ref[...], (((1,), (1,)), ((), ())), preferred_element_type=F32
        )
    else:
        out_ref[...] = dot_wide(coeffs, field_ref[...])


def turn_kernel(_, field_ref, out_ref):
    out_ref[...] = field_ref[...].T


def map_kernel(*refs, samples, others, has_factor, last):
    refs = list(refs)
    place, grp = refs.pop(0)[0], others + 1
    mapped = refs.pop(0)[...]
    modes, points = mapped.shape
    block = points // grp
    for k in range(others):
        other = refs.pop(0)[...]
        cut = (others - k) * block
        mapped = mapped + jnp.concatenate([other[:, cut:], other[:, :cut]], axis=1)
    factor = refs.pop(0)[...][:, :modes] if has_factor else None
    weight = refs.pop(0)[:1]
    if has_factor:
        mapped = jnp.dot(factor, mapped, precision=HIGHEST, preferred_element_type=F32)
    mapped = mapped * weight / samples
    padded = jnp.concatenate([mapped, jnp.zeros((LANES - modes, points), F32)], axis=0)
    gram = lax.dot_general(
        mapped, padded, (((1,), (1,)), ((), ())), precision=HIGHEST, preferred_element_type=F32
    )
    tile = fold(gram, modes)
    if last:
        out_ref, send_ref = refs
        out_ref[...] = mapped[:, :block]
        slab = own_slab(tile, place, grp)
        for d in range(send_ref.shape[0]):
            send_ref[d] = slab
        return
    field_ref, send_ref = refs
    pitch = ROWS + 1
    store_tiles(send_ref, dot_wide(mapped * weight, field_ref[...]), pitch)
    for d in range(send_ref.shape[0] // pitch):
        send_ref[d * pitch + ROWS : (d + 1) * pitch] = tile[d % ROWS : d % ROWS + 1]


def finish_kernel(place_ref, recv_ref, mapped_ref, out_ref, *, grp, pts, points):
    total = whole_tile(lambda d: recv_ref[d], place_ref[1] * (grp * pts), grp, pts)
    mapped = mapped_ref[...]
    modes = mapped.shape[0]
    factor = inverse_factor(unfold(total, modes) / points, modes)[:, :modes]
    out_ref[...] = jnp.dot(factor, mapped, precision=HIGHEST, preferred_element_type=F32)


def call(kernel, outs, *args):
    specs = [SMEM if a.dtype == jnp.int32 else VMEM for a in args]
    args = [
        a if a.dtype == jnp.int32 else pltpu.with_memory_space_constraint(a, pltpu.VMEM)
        for a in args
    ]
    out = [o if isinstance(o, jax.ShapeDtypeStruct) else pltpu.VMEM(*o) for o in outs]
    result = pl.pallas_call(
        kernel, out_shape=out, in_specs=specs, out_specs=[VMEM for _ in out]
    )(*args)
    return result if len(out) > 1 else result[0]


def cut(place, fields, weight, modes, grp):
    _, points, samples = fields.shape
    out = [pltpu.VMEM((modes.shape[1] + ROWS, points), F32)]
    out += [pltpu.VMEM((points, samples // grp), fields.dtype) for _ in range(grp)]
    anywhere = pl.BlockSpec(memory_space=pl.ANY)
    return pl.pallas_call(
        setup_kernel,
        out_shape=out,
        in_specs=[SMEM, anywhere, anywhere, anywhere],
        out_specs=[VMEM for _ in out],
        scratch_shapes=[pltpu.VMEM((1, points), F32), pltpu.SemaphoreType.DMA((grp + 2,))],
    )(place, fields, weight, modes)


def exchange(value, pitch=None):
    if pitch is None:
        return lax.all_to_all(value, ALL, 0, 0)
    chunks = value.shape[0] // pitch
    unit = ROWS if pitch == ROWS else 1
    split = value.reshape(chunks, pitch // unit, unit, LANES)
    return lax.all_to_all(split, ALL, 0, 0).reshape(value.shape)


def shifted(value, shift):
    grp = lax.axis_size("grp")
    return lax.ppermute(value, "grp", [((i + shift) % grp, i) for i in range(grp)])


def body_tiles(fields, point_weight, start_modes):
    modes, samples = start_modes.shape[1], fields.shape[2]
    grp, pts = lax.axis_size("grp"), lax.axis_size("pts")
    devices = 2 * grp * pts
    total_points = fields.shape[1] * grp * pts
    points = fields.shape[1] * grp
    place = jnp.stack([lax.axis_index("grp"), lax.axis_index("side")]).astype(jnp.int32)

    pack, *blocks = cut(place, fields, point_weight, start_modes, grp)
    packs = [pack] + [shifted(pack, k) for k in range(1, grp)]
    field = jnp.concatenate(
        [blocks[0]] + [shifted(blocks[k], k) for k in range(1, grp)], axis=0
    )
    factor, pitch = None, ROWS
    outs = [((devices * ROWS, LANES), F32), ((ROWS, points), F32)]
    send, weight = call(first_kernel, outs, *packs, field)
    for iteration in range(ITERS):
        has_gram, last = iteration > 0, iteration == ITERS - 1
        kernel = lambda *refs: reduce_kernel(*refs, grp=grp, pts=pts, pitch=pitch)
        dtype = F32 if has_gram else BF16
        summed = call(kernel, [((devices * pitch, LANES), dtype)], exchange(send, pitch))
        gathered = exchange(summed, pitch)
        kernel = lambda *refs: back_kernel(*refs, pitch=pitch, samples=samples // grp)
        own = call(
            kernel, [((modes, points), F32)], gathered, turned if has_gram else field
        )
        if not has_gram:
            shape = (field.shape[1], points)
            turned = call(turn_kernel, [(shape, field.dtype)], own, field)
        others = [shifted(own, k) for k in range(1, grp)]
        if has_gram:
            kernel = lambda *refs: factor_kernel(
                *refs, modes=modes, points=total_points, pitch=pitch
            )
            factor = call(kernel, [((modes, LANES), F32)], gathered)
        pitch = ROWS + 1
        kernel = lambda *refs: map_kernel(
            *refs, samples=samples, others=grp - 1, has_factor=has_gram, last=last
        )
        given = [place, own, *others, *([factor] if has_gram else []), weight]
        if last:
            outs = [((modes, points // grp), F32), ((devices, ROWS // grp, LANES), F32)]
            mapped, send = call(kernel, outs, *given)
        else:
            send = call(kernel, [((devices * pitch, LANES), F32)], *given, field)
    kernel = lambda *refs: finish_kernel(*refs, grp=grp, pts=pts, points=total_points)
    out = jax.ShapeDtypeStruct((modes, points // grp), F32)
    return call(kernel, [out], place, exchange(send), mapped)[None]


def body_sums(fields, point_weight, start_modes):
    local_field, weight, mode_rows = fields[0], point_weight[0], start_modes[0]
    samples = local_field.shape[1]
    total_points = local_field.shape[0] * lax.axis_size("grp") * lax.axis_size("pts")
    for _ in range(ITERS):
        weighted = (mode_rows * weight[None, :]).astype(BF16)
        partial = jnp.dot(weighted, local_field, preferred_element_type=F32)
        coeffs = lax.psum(partial, ("grp", "pts")).astype(BF16)
        partner = lax.ppermute(coeffs, "side", [(0, 1), (1, 0)])
        mapped = lax.dot_general(
            partner, local_field, (((1,), (1,)), ((), ())), preferred_element_type=F32
        )
        mapped = mapped * weight[None, :] / samples
        gram = jnp.dot(mapped, mapped.T, precision=HIGHEST, preferred_element_type=F32)
        gram = lax.psum(gram, ("grp", "pts")) / total_points
        factor = jnp.linalg.cholesky(gram)
        mode_rows = lax.linalg.triangular_solve(factor, mapped, left_side=True, lower=True)
    return mode_rows[None]


def solution(mesh):
    grp, pts = mesh.shape["grp"], mesh.shape["pts"]

    def run(fields, point_weight, start_modes):
        modes, samples = start_modes.shape[1], fields.shape[2]
        tiles = (modes // ROWS) * (samples // (LANES * grp))
        fits = tiles == 2 * grp * pts and 4 * modes == LANES and ROWS % grp == 0
        placed = (
            P("side", ("grp", "pts"), None),
            P("side", ("grp", "pts")),
            P("side", None, ("grp", "pts")),
        )
        return jax.shard_map(
            body_tiles if fits else body_sums,
            mesh=mesh,
            in_specs=placed,
            out_specs=P("side", None, ("grp", "pts")),
            check_vma=False,
        )(fields, point_weight, start_modes)

    return run
```

```python
import jax
import jax.numpy as jnp
from jax import lax
from jax.experimental import pallas as pl
from jax.experimental.pallas import tpu as pltpu
from jax.sharding import PartitionSpec as P

ITERS = 6
ROWS, LANES = 8, 128
ALL = ("side", "grp", "pts")
F32, BF16 = jnp.float32, jnp.bfloat16
HIGHEST = lax.Precision.HIGHEST
VMEM = pl.BlockSpec(memory_space=pltpu.VMEM)
SMEM = pl.BlockSpec(memory_space=pltpu.SMEM)
GRANT = pltpu.CompilerParams(vmem_limit_bytes=8 << 20)


def split3(x):
    high = x.astype(BF16)
    rest = x - high.astype(F32)
    mid = rest.astype(BF16)
    low = (rest - mid.astype(F32)).astype(BF16)
    return jnp.concatenate([high, mid, low], axis=0)


def dot_wide(x, field):
    count = x.shape[0]
    out = jnp.dot(split3(x), field, preferred_element_type=F32)
    return out[2 * count :] + out[count : 2 * count] + out[:count]


def fold(gram, modes):
    return sum(
        pltpu.roll(gram[g * ROWS : (g + 1) * ROWS], g * modes, 1) if g else gram[:ROWS]
        for g in range(modes // ROWS)
    )


def unfold(tile, modes):
    lane = lax.broadcasted_iota(jnp.int32, (ROWS, LANES), 1)
    parts = [
        pltpu.roll(tile, LANES - g * modes, 1) if g else tile for g in range(modes // ROWS)
    ]
    return jnp.concatenate([jnp.where(lane < modes, part, 0.0) for part in parts], axis=0)


def inverse_factor(gram, modes):
    row = lax.broadcasted_iota(jnp.int32, (modes, LANES), 0)
    lane = lax.broadcasted_iota(jnp.int32, (modes, LANES), 1)
    work = gram + jnp.where(lane == row + modes, 1.0, 0.0)
    for k in range(0, modes, ROWS):
        rows = [work[k + j : k + j + 1] for j in range(ROWS)]
        columns = [
            jnp.broadcast_to(work[:, k + j : k + j + 1], (modes, LANES)) for j in range(ROWS)
        ]
        block = {
            (i, j): jnp.broadcast_to(rows[i][:, k + j : k + j + 1], (1, LANES))
            for i in range(ROWS)
            for j in range(i, ROWS)
        }
        factors = []
        for j in range(ROWS):
            inverse = 1.0 / block[j, j]
            factor = jnp.where(row > k + j, columns[j] * inverse, 0.0)
            factors.append(factor)
            for i in range(j + 1, ROWS):
                columns[i] = columns[i] - factor * block[j, i]
                ratio = block[j, i] * inverse
                for c in range(i, ROWS):
                    block[i, c] = block[i, c] - ratio * block[j, c]
                rows[i] = rows[i] - ratio * rows[j]
        for j in range(ROWS):
            work = work - factors[j] * rows[j]
    pivots = jnp.sum(jnp.where(lane == row, work, 0.0), axis=1, keepdims=True)
    inverse = pltpu.roll(work, LANES - modes, 1) / jnp.sqrt(pivots)
    return jnp.where(lane < modes, inverse, 0.0)


def store_tiles(send_ref, projected, pitch):
    columns = projected.shape[1] // LANES
    for d in range(send_ref.shape[0] // pitch):
        h, j = divmod(d, columns)
        send_ref[d * pitch : d * pitch + ROWS] = projected[
            h * ROWS : (h + 1) * ROWS, j * LANES : (j + 1) * LANES
        ]


def own_slab(tile, place, grp):
    slab = ROWS // grp
    return sum(
        jnp.where(place == c, tile[c * slab : (c + 1) * slab], 0.0) for c in range(grp)
    )


def whole_tile(read, first, grp, pts):
    slabs = []
    for c in range(grp):
        total = read(first + c * pts)
        for p in range(1, pts):
            total = total + read(first + c * pts + p)
        slabs.append(total)
    return jnp.concatenate(slabs, axis=0)


def setup_kernel(place_ref, _, fields_ref, weight_ref, modes_ref, pack_ref, *rest):
    *block_refs, row_ref, sems = rest
    grp, columns = len(block_refs), block_refs[0].shape[1]
    modes = modes_ref.shape[1]
    pairs = [(weight_ref, row_ref), (modes_ref.at[0], pack_ref.at[:modes])]
    for k in reversed(range(grp)):
        start = pl.multiple_of(lax.rem(place_ref[0] + grp - k, grp) * columns, LANES)
        pairs.append((fields_ref.at[0, :, pl.ds(start, columns)], block_refs[k]))
    copies = [
        pltpu.make_async_copy(source, target, sems.at[i])
        for i, (source, target) in enumerate(pairs)
    ]
    for copy in copies:
        copy.start()
    copies[0].wait()
    pack_ref[modes:] = jnp.broadcast_to(row_ref[...], (ROWS, row_ref.shape[1]))
    for copy in copies[1:]:
        copy.wait()


def first_kernel(*refs):
    *pack_refs, field_ref, send_ref, weight_ref = refs
    pack = jnp.concatenate([ref[...] for ref in pack_refs], axis=1)
    weight = pack[-ROWS:]
    weight_ref[...] = weight
    store_tiles(send_ref, dot_wide(pack[:-ROWS] * weight[:1], field_ref[...]), ROWS)


def reduce_kernel(recv_ref, send_ref, *, grp, pts, pitch):
    def total(first, rows):
        parts = [recv_ref[d * pitch + rows.start : d * pitch + rows.stop] for d in
                 range(first, first + pts)]
        return sum(parts[1:], parts[0])

    for s in range(2):
        gram = total(s * grp * pts, slice(ROWS, pitch)) if pitch > ROWS else None
        for c in range(grp):
            tile = total((s * grp + c) * pts, slice(0, ROWS)).astype(send_ref.dtype)
            for p in range(pts):
                first = (((1 - s) * grp + c) * pts + p) * pitch
                send_ref[first : first + ROWS] = tile
                if pitch > ROWS:
                    send_ref[first + ROWS : first + pitch] = gram


def factor_kernel(recv_ref, out_ref, *, modes, points, pitch):
    gram = jnp.concatenate(
        [recv_ref[r * pitch + ROWS : (r + 1) * pitch] for r in range(ROWS)], axis=0
    )
    out_ref[...] = inverse_factor(unfold(gram, modes) / points, modes)


def back_kernel(recv_ref, field_ref, out_ref, *, pitch, samples):
    columns = samples // LANES
    count = recv_ref.shape[0] // (pitch * columns)
    coeffs = jnp.concatenate(
        [
            jnp.concatenate(
                [
                    recv_ref[(h * columns + j) * pitch : (h * columns + j) * pitch + ROWS]
                    for j in range(columns)
                ],
                axis=1,
            )
            for h in range(count)
        ],
        axis=0,
    )
    if coeffs.dtype == BF16:
        out_ref[...] = lax.dot_general(
            coeffs, field_ref[...], (((1,), (1,)), ((), ())), preferred_element_type=F32
        )
    else:
        out_ref[...] = dot_wide(coeffs, field_ref[...])


def turn_kernel(_, field_ref, out_ref):
    out_ref[...] = field_ref[...].T


def map_kernel(*refs, samples, others, has_factor, last):
    refs = list(refs)
    place, grp = refs.pop(0)[0], others + 1
    mapped = refs.pop(0)[...]
    modes, points = mapped.shape
    block = points // grp
    for k in range(others):
        other = refs.pop(0)[...]
        cut = (others - k) * block
        mapped = mapped + jnp.concatenate([other[:, cut:], other[:, :cut]], axis=1)
    factor = refs.pop(0)[...][:, :modes]
    weight = refs.pop(0)[:1]
    if has_factor:
        mapped = jnp.dot(factor, mapped, precision=HIGHEST, preferred_element_type=F32)
    mapped = mapped * weight / samples
    padded = jnp.concatenate([mapped, jnp.zeros((LANES - modes, points), F32)], axis=0)
    gram = lax.dot_general(
        mapped, padded, (((1,), (1,)), ((), ())), precision=HIGHEST, preferred_element_type=F32
    )
    tile = fold(gram, modes)
    if last:
        out_ref, send_ref = refs
        out_ref[...] = mapped[:, :block]
        slab = own_slab(tile, place, grp)
        for d in range(send_ref.shape[0]):
            send_ref[d] = slab
        return
    field_ref, send_ref = refs
    pitch = ROWS + 1
    store_tiles(send_ref, dot_wide(mapped * weight, field_ref[...]), pitch)
    for d in range(send_ref.shape[0] // pitch):
        send_ref[d * pitch + ROWS : (d + 1) * pitch] = tile[d % ROWS : d % ROWS + 1]


def finish_kernel(side_ref, recv_ref, mapped_ref, out_ref, *, grp, pts, points):
    total = whole_tile(lambda d: recv_ref[d], side_ref[0] * (grp * pts), grp, pts)
    mapped = mapped_ref[...]
    modes = mapped.shape[0]
    factor = inverse_factor(unfold(total, modes) / points, modes)[:, :modes]
    out_ref[...] = jnp.dot(factor, mapped, precision=HIGHEST, preferred_element_type=F32)


def call(kernel, outs, *args):
    specs = [SMEM if a.dtype == jnp.int32 else VMEM for a in args]
    args = [
        a if a.dtype == jnp.int32 else pltpu.with_memory_space_constraint(a, pltpu.VMEM)
        for a in args
    ]
    out = [o if isinstance(o, jax.ShapeDtypeStruct) else pltpu.VMEM(*o) for o in outs]
    result = pl.pallas_call(
        kernel,
        out_shape=out,
        in_specs=specs,
        out_specs=[VMEM for _ in out],
        compiler_params=GRANT,
    )(*args)
    return result if len(out) > 1 else result[0]


def cut(place, side, fields, weight, modes, grp):
    _, points, samples = fields.shape
    out = [pltpu.VMEM((modes.shape[1] + ROWS, points), F32)]
    out += [pltpu.VMEM((points, samples // grp), fields.dtype) for _ in range(grp)]
    anywhere = pl.BlockSpec(memory_space=pltpu.HBM)
    return pl.pallas_call(
        setup_kernel,
        out_shape=out,
        in_specs=[SMEM, SMEM, anywhere, anywhere, anywhere],
        out_specs=[VMEM for _ in out],
        compiler_params=GRANT,
        scratch_shapes=[pltpu.VMEM((1, points), F32), pltpu.SemaphoreType.DMA((grp + 2,))],
    )(place, side, *(pltpu.with_memory_space_constraint(a, pltpu.HBM) for a in (fields, weight, modes)))


def exchange(value, pitch=None):
    if pitch is None:
        return lax.all_to_all(value, ALL, 0, 0)
    chunks = value.shape[0] // pitch
    unit = ROWS if pitch == ROWS else 1
    split = value.reshape(chunks, pitch // unit, unit, LANES)
    return lax.all_to_all(split, ALL, 0, 0).reshape(value.shape)


def shifted(value, shift):
    grp = lax.axis_size("grp")
    return lax.ppermute(value, "grp", [((i + shift) % grp, i) for i in range(grp)])


def body_tiles(fields, point_weight, start_modes):
    modes, samples = start_modes.shape[1], fields.shape[2]
    grp, pts = lax.axis_size("grp"), lax.axis_size("pts")
    devices = 2 * grp * pts
    total_points = fields.shape[1] * grp * pts
    points = fields.shape[1] * grp
    place = lax.axis_index("grp").astype(jnp.int32).reshape(1)
    side = lax.axis_index("side").astype(jnp.int32).reshape(1)

    pack, *blocks = cut(place, side, fields, point_weight, start_modes, grp)
    packs = [pack] + [shifted(pack, k) for k in range(1, grp)]
    field = jnp.concatenate(
        [blocks[0]] + [shifted(blocks[k], k) for k in range(1, grp)], axis=0
    )
    factor, pitch = None, ROWS
    outs = [((devices * ROWS, LANES), F32), ((ROWS, points), F32)]
    send, weight = call(first_kernel, outs, *packs, field)
    for iteration in range(ITERS):
        has_gram, last = iteration > 0, iteration == ITERS - 1
        kernel = lambda *refs: reduce_kernel(*refs, grp=grp, pts=pts, pitch=pitch)
        dtype = F32 if has_gram else BF16
        summed = call(kernel, [((devices * pitch, LANES), dtype)], exchange(send, pitch))
        gathered = exchange(summed, pitch)
        kernel = lambda *refs: back_kernel(*refs, pitch=pitch, samples=samples // grp)
        own = call(
            kernel, [((modes, points), F32)], gathered, turned if has_gram else field
        )
        if not has_gram:
            shape = (field.shape[1], points)
            turned = call(turn_kernel, [(shape, field.dtype)], own, field)
        others = [shifted(own, k) for k in range(1, grp)]
        if has_gram:
            kernel = lambda *refs: factor_kernel(
                *refs, modes=modes, points=total_points, pitch=pitch
            )
            factor = call(kernel, [((modes, LANES), F32)], gathered)
        pitch = ROWS + 1
        kernel = lambda *refs: map_kernel(
            *refs, samples=samples, others=grp - 1, has_factor=has_gram, last=last
        )
        given = [place, own, *others, factor if has_gram else turned, weight]
        if last:
            outs = [((modes, points // grp), F32), ((devices, ROWS // grp, LANES), F32)]
            mapped, send = call(kernel, outs, *given)
        else:
            send = call(kernel, [((devices * pitch, LANES), F32)], *given, field)
    kernel = lambda *refs: finish_kernel(*refs, grp=grp, pts=pts, points=total_points)
    out = jax.ShapeDtypeStruct((modes, points // grp), F32)
    return call(kernel, [out], side, exchange(send), mapped)[None]


def body_sums(fields, point_weight, start_modes):
    local_field, weight, mode_rows = fields[0], point_weight[0], start_modes[0]
    samples = local_field.shape[1]
    total_points = local_field.shape[0] * lax.axis_size("grp") * lax.axis_size("pts")
    for _ in range(ITERS):
        weighted = (mode_rows * weight[None, :]).astype(BF16)
        partial = jnp.dot(weighted, local_field, preferred_element_type=F32)
        coeffs = lax.psum(partial, ("grp", "pts")).astype(BF16)
        partner = lax.ppermute(coeffs, "side", [(0, 1), (1, 0)])
        mapped = lax.dot_general(
            partner, local_field, (((1,), (1,)), ((), ())), preferred_element_type=F32
        )
        mapped = mapped * weight[None, :] / samples
        gram = jnp.dot(mapped, mapped.T, precision=HIGHEST, preferred_element_type=F32)
        gram = lax.psum(gram, ("grp", "pts")) / total_points
        factor = jnp.linalg.cholesky(gram)
        mode_rows = lax.linalg.triangular_solve(factor, mapped, left_side=True, lower=True)
    return mode_rows[None]


def solution(mesh):
    grp, pts = mesh.shape["grp"], mesh.shape["pts"]

    def run(fields, point_weight, start_modes):
        modes, samples = start_modes.shape[1], fields.shape[2]
        tiles = (modes // ROWS) * (samples // (LANES * grp))
        fits = tiles == 2 * grp * pts and 4 * modes == LANES and ROWS % grp == 0
        placed = (
            P("side", ("grp", "pts"), None),
            P("side", ("grp", "pts")),
            P("side", None, ("grp", "pts")),
        )
        return jax.shard_map(
            body_tiles if fits else body_sums,
            mesh=mesh,
            in_specs=placed,
            out_specs=P("side", None, ("grp", "pts")),
            check_vma=False,
        )(fields, point_weight, start_modes)

    return run
```

```python
import jax
import jax.numpy as jnp
from jax import lax
from jax.experimental import pallas as pl
from jax.experimental.pallas import tpu as pltpu
from jax.sharding import PartitionSpec as P

ITERS = 6
ROWS, LANES = 8, 128
ALL = ("side", "grp", "pts")
F32, BF16 = jnp.float32, jnp.bfloat16
HIGHEST = lax.Precision.HIGHEST
VMEM = pl.BlockSpec(memory_space=pltpu.VMEM)
SMEM = pl.BlockSpec(memory_space=pltpu.SMEM)
GRANT = pltpu.CompilerParams(vmem_limit_bytes=8 << 20)


def split3(x):
    high = x.astype(BF16)
    rest = x - high.astype(F32)
    mid = rest.astype(BF16)
    low = (rest - mid.astype(F32)).astype(BF16)
    return jnp.concatenate([high, mid, low], axis=0)


def dot_wide(x, field):
    count = x.shape[0]
    out = jnp.dot(split3(x), field, preferred_element_type=F32)
    return out[2 * count :] + out[count : 2 * count] + out[:count]


def fold(gram, modes):
    return sum(
        pltpu.roll(gram[g * ROWS : (g + 1) * ROWS], g * modes, 1) if g else gram[:ROWS]
        for g in range(modes // ROWS)
    )


def unfold(tile, modes):
    lane = lax.broadcasted_iota(jnp.int32, (ROWS, LANES), 1)
    parts = [
        pltpu.roll(tile, LANES - g * modes, 1) if g else tile for g in range(modes // ROWS)
    ]
    return jnp.concatenate([jnp.where(lane < modes, part, 0.0) for part in parts], axis=0)


def inverse_factor(gram, modes):
    row = lax.broadcasted_iota(jnp.int32, (modes, LANES), 0)
    lane = lax.broadcasted_iota(jnp.int32, (modes, LANES), 1)
    work = gram + jnp.where(lane == row + modes, 1.0, 0.0)
    for k in range(0, modes, ROWS):
        rows = [work[k + j : k + j + 1] for j in range(ROWS)]
        columns = [
            jnp.broadcast_to(work[:, k + j : k + j + 1], (modes, LANES)) for j in range(ROWS)
        ]
        block = {
            (i, j): jnp.broadcast_to(rows[i][:, k + j : k + j + 1], (1, LANES))
            for i in range(ROWS)
            for j in range(i, ROWS)
        }
        factors = []
        for j in range(ROWS):
            inverse = 1.0 / block[j, j]
            factor = jnp.where(row > k + j, columns[j] * inverse, 0.0)
            factors.append(factor)
            for i in range(j + 1, ROWS):
                columns[i] = columns[i] - factor * block[j, i]
                ratio = block[j, i] * inverse
                for c in range(i, ROWS):
                    block[i, c] = block[i, c] - ratio * block[j, c]
                rows[i] = rows[i] - ratio * rows[j]
        for j in range(ROWS):
            work = work - factors[j] * rows[j]
    pivots = jnp.sum(jnp.where(lane == row, work, 0.0), axis=1, keepdims=True)
    inverse = pltpu.roll(work, LANES - modes, 1) / jnp.sqrt(pivots)
    return jnp.where(lane < modes, inverse, 0.0)


def store_tiles(send_ref, projected, pitch):
    columns = projected.shape[1] // LANES
    for d in range(send_ref.shape[0] // pitch):
        h, j = divmod(d, columns)
        send_ref[d * pitch : d * pitch + ROWS] = projected[
            h * ROWS : (h + 1) * ROWS, j * LANES : (j + 1) * LANES
        ]


def own_slab(tile, place, grp):
    slab = ROWS // grp
    return sum(
        jnp.where(place == c, tile[c * slab : (c + 1) * slab], 0.0) for c in range(grp)
    )


def whole_tile(read, first, grp, pts):
    slabs = []
    for c in range(grp):
        total = read(first + c * pts)
        for p in range(1, pts):
            total = total + read(first + c * pts + p)
        slabs.append(total)
    return jnp.concatenate(slabs, axis=0)


def start_kernel(place_ref, _, fields_ref, weight_ref, modes_ref, weights_ref, part_ref, *rest):
    *out_refs, row_ref, modes_vmem, sems = rest
    grp = (len(out_refs) + 1) // 2
    part_refs, block_refs = [part_ref] + out_refs[: grp - 1], out_refs[grp - 1 :]
    columns, modes = block_refs[0].shape[1], part_ref.shape[0]
    pairs = [(weight_ref, row_ref), (modes_ref.at[0], modes_vmem)]
    order = list(reversed(range(grp)))
    for k in order:
        start = pl.multiple_of(lax.rem(place_ref[0] + grp - k, grp) * columns, LANES)
        pairs.append((fields_ref.at[0, :, pl.ds(start, columns)], block_refs[k]))
    copies = [
        pltpu.make_async_copy(source, target, sems.at[i])
        for i, (source, target) in enumerate(pairs)
    ]
    for copy in copies:
        copy.start()
    copies[0].wait()
    copies[1].wait()
    weights = jnp.broadcast_to(row_ref[...], weights_ref.shape)
    weights_ref[...] = weights
    weighted = modes_vmem[...] * row_ref[...]
    for k, copy in zip(order, copies[2:]):
        if k:
            part_refs[k][modes:, : weights.shape[1]] = weights
            part_refs[k][modes:, weights.shape[1] :] = jnp.zeros(
                (ROWS, columns - weights.shape[1]), F32
            )
        copy.wait()
        part_refs[k][:modes] = dot_wide(weighted, block_refs[k][...])


def first_kernel(weights_ref, part_ref, *refs):
    *message_refs, send_ref, weight_ref = refs
    modes, points = part_ref.shape[0], weights_ref.shape[1]
    total, weights = part_ref[...], [weights_ref[...]]
    for ref in message_refs:
        total = total + ref[:modes]
        weights.append(ref[modes:, :points])
    store_tiles(send_ref, total, ROWS)
    weight_ref[...] = jnp.concatenate(weights, axis=1)


def reduce_kernel(recv_ref, send_ref, *, grp, pts, pitch):
    def total(first, rows):
        parts = [recv_ref[d * pitch + rows.start : d * pitch + rows.stop] for d in
                 range(first, first + pts)]
        return sum(parts[1:], parts[0])

    for s in range(2):
        gram = total(s * grp * pts, slice(ROWS, pitch)) if pitch > ROWS else None
        for c in range(grp):
            tile = total((s * grp + c) * pts, slice(0, ROWS)).astype(send_ref.dtype)
            for p in range(pts):
                first = (((1 - s) * grp + c) * pts + p) * pitch
                send_ref[first : first + ROWS] = tile
                if pitch > ROWS:
                    send_ref[first + ROWS : first + pitch] = gram


def factor_kernel(recv_ref, out_ref, *, modes, points, pitch):
    gram = jnp.concatenate(
        [recv_ref[r * pitch + ROWS : (r + 1) * pitch] for r in range(ROWS)], axis=0
    )
    out_ref[...] = inverse_factor(unfold(gram, modes) / points, modes)


def gathered_rows(recv_ref, columns, pitch):
    count = recv_ref.shape[0] // (pitch * columns)
    return jnp.concatenate(
        [
            jnp.concatenate(
                [
                    recv_ref[(h * columns + j) * pitch : (h * columns + j) * pitch + ROWS]
                    for j in range(columns)
                ],
                axis=1,
            )
            for h in range(count)
        ],
        axis=0,
    )


def first_back_kernel(recv_ref, *refs):
    *block_refs, out_ref = refs
    coeffs = gathered_rows(recv_ref, block_refs[0].shape[1] // LANES, ROWS)
    points = block_refs[0].shape[0]
    for k, ref in enumerate(block_refs):
        out_ref[:, k * points : (k + 1) * points] = lax.dot_general(
            coeffs, ref[...], (((1,), (1,)), ((), ())), preferred_element_type=F32
        )


def back_kernel(recv_ref, turned_ref, out_ref, *, pitch):
    coeffs = gathered_rows(recv_ref, turned_ref.shape[0] // LANES, pitch)
    out_ref[...] = dot_wide(coeffs, turned_ref[...])


def join_kernel(_, *refs):
    *block_refs, field_ref, turned_ref = refs
    points = block_refs[0].shape[0]
    for k, ref in enumerate(block_refs):
        field_ref[k * points : (k + 1) * points] = ref[...]
        turned_ref[:, k * points : (k + 1) * points] = ref[...].T


def map_kernel(*refs, samples, others, has_factor, last):
    refs = list(refs)
    place, grp = refs.pop(0)[0], others + 1
    mapped = refs.pop(0)[...]
    modes, points = mapped.shape
    block = points // grp
    for k in range(others):
        other = refs.pop(0)[...]
        cut = (others - k) * block
        mapped = mapped + jnp.concatenate([other[:, cut:], other[:, :cut]], axis=1)
    factor = refs.pop(0)[...][:, :modes] if has_factor else None
    weight = refs.pop(0)[:1]
    if has_factor:
        mapped = jnp.dot(factor, mapped, precision=HIGHEST, preferred_element_type=F32)
    mapped = mapped * weight / samples
    padded = jnp.concatenate([mapped, jnp.zeros((LANES - modes, points), F32)], axis=0)
    gram = lax.dot_general(
        mapped, padded, (((1,), (1,)), ((), ())), precision=HIGHEST, preferred_element_type=F32
    )
    tile = fold(gram, modes)
    if last:
        out_ref, send_ref = refs
        out_ref[...] = mapped[:, :block]
        slab = own_slab(tile, place, grp)
        for d in range(send_ref.shape[0]):
            send_ref[d] = slab
        return
    field_ref, send_ref = refs
    pitch = ROWS + 1
    store_tiles(send_ref, dot_wide(mapped * weight, field_ref[...]), pitch)
    for d in range(send_ref.shape[0] // pitch):
        send_ref[d * pitch + ROWS : (d + 1) * pitch] = tile[d % ROWS : d % ROWS + 1]


def finish_kernel(side_ref, recv_ref, mapped_ref, out_ref, *, grp, pts, points):
    total = whole_tile(lambda d: recv_ref[d], side_ref[0] * (grp * pts), grp, pts)
    mapped = mapped_ref[...]
    modes = mapped.shape[0]
    factor = inverse_factor(unfold(total, modes) / points, modes)[:, :modes]
    out_ref[...] = jnp.dot(factor, mapped, precision=HIGHEST, preferred_element_type=F32)


def call(kernel, outs, *args):
    specs = [SMEM if a.dtype == jnp.int32 else VMEM for a in args]
    args = [
        a if a.dtype == jnp.int32 else pltpu.with_memory_space_constraint(a, pltpu.VMEM)
        for a in args
    ]
    out = [o if isinstance(o, jax.ShapeDtypeStruct) else pltpu.VMEM(*o) for o in outs]
    result = pl.pallas_call(
        kernel,
        out_shape=out,
        in_specs=specs,
        out_specs=[VMEM for _ in out],
        compiler_params=GRANT,
    )(*args)
    return result if len(out) > 1 else result[0]


def begin(place, side, fields, weight, modes, grp):
    _, points, samples = fields.shape
    columns, rows = samples // grp, modes.shape[1]
    out = [pltpu.VMEM((ROWS, points), F32), pltpu.VMEM((rows, columns), F32)]
    out += [pltpu.VMEM((rows + ROWS, columns), F32) for _ in range(1, grp)]
    out += [pltpu.VMEM((points, columns), fields.dtype) for _ in range(grp)]
    far = [pltpu.with_memory_space_constraint(a, pltpu.HBM) for a in (fields, weight, modes)]
    weights, part, *rest = pl.pallas_call(
        start_kernel,
        out_shape=out,
        in_specs=[SMEM, SMEM] + [pl.BlockSpec(memory_space=pltpu.HBM)] * 3,
        out_specs=[VMEM for _ in out],
        compiler_params=GRANT,
        scratch_shapes=[
            pltpu.VMEM((1, points), F32),
            pltpu.VMEM((rows, points), F32),
            pltpu.SemaphoreType.DMA((grp + 2,)),
        ],
    )(place, side, *far)
    return weights, part, rest[: grp - 1], rest[grp - 1 :]


def exchange(value, pitch=None):
    if pitch is None:
        return lax.all_to_all(value, ALL, 0, 0)
    chunks = value.shape[0] // pitch
    unit = ROWS if pitch == ROWS else 1
    split = value.reshape(chunks, pitch // unit, unit, LANES)
    return lax.all_to_all(split, ALL, 0, 0).reshape(value.shape)


def shifted(value, shift):
    grp = lax.axis_size("grp")
    return lax.ppermute(value, "grp", [((i + shift) % grp, i) for i in range(grp)])


def body_tiles(fields, point_weight, start_modes):
    modes, samples = start_modes.shape[1], fields.shape[2]
    grp, pts = lax.axis_size("grp"), lax.axis_size("pts")
    devices = 2 * grp * pts
    total_points = fields.shape[1] * grp * pts
    points = fields.shape[1] * grp
    place = lax.axis_index("grp").astype(jnp.int32).reshape(1)
    side = lax.axis_index("side").astype(jnp.int32).reshape(1)

    weights, part, messages, blocks = begin(
        place, side, fields, point_weight, start_modes, grp
    )
    messages = [shifted(m, k + 1) for k, m in enumerate(messages)]
    *others, _ = lax.optimization_barrier((*blocks[1:], messages))
    blocks = [blocks[0]] + [shifted(block, k + 1) for k, block in enumerate(others)]
    pitch = ROWS
    outs = [((devices * ROWS, LANES), F32), ((ROWS, points), F32)]
    send, weight = call(first_kernel, outs, weights, part, *messages)
    for iteration in range(ITERS):
        has_gram, last = iteration > 0, iteration == ITERS - 1
        kernel = lambda *refs: reduce_kernel(*refs, grp=grp, pts=pts, pitch=pitch)
        dtype = F32 if has_gram else BF16
        summed = call(kernel, [((devices * pitch, LANES), dtype)], exchange(send, pitch))
        gathered = exchange(summed, pitch)
        outs = [((modes, points), F32)]
        if has_gram:
            kernel = lambda *refs: back_kernel(*refs, pitch=pitch)
            own = call(kernel, outs, gathered, turned)
            kernel = lambda *refs: factor_kernel(
                *refs, modes=modes, points=total_points, pitch=pitch
            )
            factor = [call(kernel, [((modes, LANES), F32)], gathered)]
        else:
            own = call(first_back_kernel, outs, gathered, *blocks)
            outs = [((points, samples // grp), BF16), ((samples // grp, points), BF16)]
            field, turned = call(join_kernel, outs, own, *blocks)
            factor = []
        others = [shifted(own, k) for k in range(1, grp)]
        pitch = ROWS + 1
        kernel = lambda *refs: map_kernel(
            *refs, samples=samples, others=grp - 1, has_factor=has_gram, last=last
        )
        given = [place, own, *others, *factor, weight]
        if last:
            outs = [((modes, points // grp), F32), ((devices, ROWS // grp, LANES), F32)]
            mapped, send = call(kernel, outs, *given)
        else:
            send = call(kernel, [((devices * pitch, LANES), F32)], *given, field)
    kernel = lambda *refs: finish_kernel(*refs, grp=grp, pts=pts, points=total_points)
    out = jax.ShapeDtypeStruct((modes, points // grp), F32)
    return call(kernel, [out], side, exchange(send), mapped)[None]


def body_sums(fields, point_weight, start_modes):
    local_field, weight, mode_rows = fields[0], point_weight[0], start_modes[0]
    samples = local_field.shape[1]
    total_points = local_field.shape[0] * lax.axis_size("grp") * lax.axis_size("pts")
    for _ in range(ITERS):
        weighted = (mode_rows * weight[None, :]).astype(BF16)
        partial = jnp.dot(weighted, local_field, preferred_element_type=F32)
        coeffs = lax.psum(partial, ("grp", "pts")).astype(BF16)
        partner = lax.ppermute(coeffs, "side", [(0, 1), (1, 0)])
        mapped = lax.dot_general(
            partner, local_field, (((1,), (1,)), ((), ())), preferred_element_type=F32
        )
        mapped = mapped * weight[None, :] / samples
        gram = jnp.dot(mapped, mapped.T, precision=HIGHEST, preferred_element_type=F32)
        gram = lax.psum(gram, ("grp", "pts")) / total_points
        factor = jnp.linalg.cholesky(gram)
        mode_rows = lax.linalg.triangular_solve(factor, mapped, left_side=True, lower=True)
    return mode_rows[None]


def solution(mesh):
    grp, pts = mesh.shape["grp"], mesh.shape["pts"]

    def run(fields, point_weight, start_modes):
        modes, samples = start_modes.shape[1], fields.shape[2]
        tiles = (modes // ROWS) * (samples // (LANES * grp))
        fits = tiles == 2 * grp * pts and 4 * modes == LANES and ROWS % grp == 0
        fits = fits and fields.shape[1] <= samples * pts
        placed = (
            P("side", ("grp", "pts"), None),
            P("side", ("grp", "pts")),
            P("side", None, ("grp", "pts")),
        )
        return jax.shard_map(
            body_tiles if fits else body_sums,
            mesh=mesh,
            in_specs=placed,
            out_specs=P("side", None, ("grp", "pts")),
            check_vma=False,
        )(fields, point_weight, start_modes)

    return run
```

```python
import jax
import jax.numpy as jnp
from jax import lax
from jax.experimental import pallas as pl
from jax.experimental.pallas import tpu as pltpu
from jax.sharding import PartitionSpec as P

ITERS = 6
ROWS, LANES = 8, 128
ALL = ("side", "grp", "pts")
F32, BF16 = jnp.float32, jnp.bfloat16
HIGHEST = lax.Precision.HIGHEST
VMEM = pl.BlockSpec(memory_space=pltpu.VMEM)
SMEM = pl.BlockSpec(memory_space=pltpu.SMEM)
GRANT = pltpu.CompilerParams(vmem_limit_bytes=8 << 20)


def split3(x):
    high = x.astype(BF16)
    rest = x - high.astype(F32)
    mid = rest.astype(BF16)
    low = (rest - mid.astype(F32)).astype(BF16)
    return jnp.concatenate([high, mid, low], axis=0)


def dot_wide(x, field):
    count = x.shape[0]
    out = jnp.dot(split3(x), field, preferred_element_type=F32)
    return out[2 * count :] + out[count : 2 * count] + out[:count]


def fold(gram, modes):
    return sum(
        pltpu.roll(gram[g * ROWS : (g + 1) * ROWS], g * modes, 1) if g else gram[:ROWS]
        for g in range(modes // ROWS)
    )


def unfold(tile, modes):
    lane = lax.broadcasted_iota(jnp.int32, (ROWS, LANES), 1)
    parts = [
        pltpu.roll(tile, LANES - g * modes, 1) if g else tile for g in range(modes // ROWS)
    ]
    return jnp.concatenate([jnp.where(lane < modes, part, 0.0) for part in parts], axis=0)


def inverse_factor(gram, modes):
    row = lax.broadcasted_iota(jnp.int32, (modes, LANES), 0)
    lane = lax.broadcasted_iota(jnp.int32, (modes, LANES), 1)
    work = gram + jnp.where(lane == row + modes, 1.0, 0.0)
    for k in range(0, modes, ROWS):
        rows = [work[k + j : k + j + 1] for j in range(ROWS)]
        columns = [
            jnp.broadcast_to(work[:, k + j : k + j + 1], (modes, LANES)) for j in range(ROWS)
        ]
        block = {
            (i, j): jnp.broadcast_to(rows[i][:, k + j : k + j + 1], (1, LANES))
            for i in range(ROWS)
            for j in range(i, ROWS)
        }
        factors = []
        for j in range(ROWS):
            inverse = 1.0 / block[j, j]
            factor = jnp.where(row > k + j, columns[j] * inverse, 0.0)
            factors.append(factor)
            for i in range(j + 1, ROWS):
                columns[i] = columns[i] - factor * block[j, i]
                ratio = block[j, i] * inverse
                for c in range(i, ROWS):
                    block[i, c] = block[i, c] - ratio * block[j, c]
                rows[i] = rows[i] - ratio * rows[j]
        for j in range(ROWS):
            work = work - factors[j] * rows[j]
    pivots = jnp.sum(jnp.where(lane == row, work, 0.0), axis=1, keepdims=True)
    inverse = pltpu.roll(work, LANES - modes, 1) / jnp.sqrt(pivots)
    return jnp.where(lane < modes, inverse, 0.0)


def store_tiles(send_ref, projected, pitch):
    columns = projected.shape[1] // LANES
    for d in range(send_ref.shape[0] // pitch):
        h, j = divmod(d, columns)
        send_ref[d * pitch : d * pitch + ROWS] = projected[
            h * ROWS : (h + 1) * ROWS, j * LANES : (j + 1) * LANES
        ]


def own_slab(tile, place, grp):
    slab = ROWS // grp
    return sum(
        jnp.where(place == c, tile[c * slab : (c + 1) * slab], 0.0) for c in range(grp)
    )


def whole_tile(read, first, grp, pts):
    slabs = []
    for c in range(grp):
        total = read(first + c * pts)
        for p in range(1, pts):
            total = total + read(first + c * pts + p)
        slabs.append(total)
    return jnp.concatenate(slabs, axis=0)


def own_part(place_ref, fields_ref, back, columns, grp):
    start = pl.multiple_of(lax.rem(place_ref[0] + grp - back, grp) * columns, LANES)
    return fields_ref.at[0, :, pl.ds(start, columns)]


def send_kernel(place_ref, _, fields_ref, weight_ref, modes_ref, weights_ref, weighted_ref, *rest):
    *out_refs, row_ref, modes_vmem, sems = rest
    others = len(out_refs) // 2
    message_refs, block_refs = out_refs[:others], out_refs[others:]
    modes = weighted_ref.shape[0]
    pairs = [(weight_ref, row_ref), (modes_ref.at[0], modes_vmem)]
    for k, ref in enumerate(block_refs):
        columns = ref.shape[1]
        pairs.append((own_part(place_ref, fields_ref, k + 1, columns, others + 1), ref))
    copies = [
        pltpu.make_async_copy(source, target, sems.at[i])
        for i, (source, target) in enumerate(pairs)
    ]
    for copy in copies:
        copy.start()
    copies[0].wait()
    copies[1].wait()
    weights = jnp.broadcast_to(row_ref[...], weights_ref.shape)
    weights_ref[...] = weights
    weighted = modes_vmem[...] * row_ref[...]
    weighted_ref[...] = weighted
    points = weights.shape[1]
    for message, block, copy in zip(message_refs, block_refs, copies[2:]):
        message[modes:, :points] = weights
        message[modes:, points:] = jnp.zeros((ROWS, message.shape[1] - points), F32)
        copy.wait()
        message[:modes] = dot_wide(weighted, block[...])


def keep_kernel(place_ref, weighted_ref, fields_ref, part_ref, block_ref, sem, *, grp):
    source = own_part(place_ref, fields_ref, 0, block_ref.shape[1], grp)
    copy = pltpu.make_async_copy(source, block_ref, sem)
    copy.start()
    copy.wait()
    part_ref[...] = dot_wide(weighted_ref[...], block_ref[...])


def first_kernel(weights_ref, part_ref, *refs):
    *message_refs, send_ref, weight_ref = refs
    modes, points = part_ref.shape[0], weights_ref.shape[1]
    total, weights = part_ref[...], [weights_ref[...]]
    for ref in message_refs:
        total = total + ref[:modes]
        weights.append(ref[modes:, :points])
    store_tiles(send_ref, total, ROWS)
    weight_ref[...] = jnp.concatenate(weights, axis=1)


def reduce_kernel(recv_ref, send_ref, *, grp, pts, pitch):
    def total(first, rows):
        parts = [recv_ref[d * pitch + rows.start : d * pitch + rows.stop] for d in
                 range(first, first + pts)]
        return sum(parts[1:], parts[0])

    for s in range(2):
        gram = total(s * grp * pts, slice(ROWS, pitch)) if pitch > ROWS else None
        for c in range(grp):
            tile = total((s * grp + c) * pts, slice(0, ROWS)).astype(send_ref.dtype)
            for p in range(pts):
                first = (((1 - s) * grp + c) * pts + p) * pitch
                send_ref[first : first + ROWS] = tile
                if pitch > ROWS:
                    send_ref[first + ROWS : first + pitch] = gram


def factor_kernel(recv_ref, out_ref, *, modes, points, pitch):
    gram = jnp.concatenate(
        [recv_ref[r * pitch + ROWS : (r + 1) * pitch] for r in range(ROWS)], axis=0
    )
    out_ref[...] = inverse_factor(unfold(gram, modes) / points, modes)


def gathered_rows(recv_ref, columns, pitch):
    count = recv_ref.shape[0] // (pitch * columns)
    return jnp.concatenate(
        [
            jnp.concatenate(
                [
                    recv_ref[(h * columns + j) * pitch : (h * columns + j) * pitch + ROWS]
                    for j in range(columns)
                ],
                axis=1,
            )
            for h in range(count)
        ],
        axis=0,
    )


def first_back_kernel(recv_ref, *refs):
    *block_refs, out_ref = refs
    coeffs = gathered_rows(recv_ref, block_refs[0].shape[1] // LANES, ROWS)
    points = block_refs[0].shape[0]
    for k, ref in enumerate(block_refs):
        out_ref[:, k * points : (k + 1) * points] = lax.dot_general(
            coeffs, ref[...], (((1,), (1,)), ((), ())), preferred_element_type=F32
        )


def back_kernel(recv_ref, turned_ref, out_ref, *, pitch):
    coeffs = gathered_rows(recv_ref, turned_ref.shape[0] // LANES, pitch)
    out_ref[...] = dot_wide(coeffs, turned_ref[...])


def join_kernel(_, *refs):
    *block_refs, field_ref, turned_ref = refs
    points = block_refs[0].shape[0]
    for k, ref in enumerate(block_refs):
        field_ref[k * points : (k + 1) * points] = ref[...]
        turned_ref[:, k * points : (k + 1) * points] = ref[...].T


def map_kernel(*refs, samples, others, has_factor, last):
    refs = list(refs)
    place, grp = refs.pop(0)[0], others + 1
    mapped = refs.pop(0)[...]
    modes, points = mapped.shape
    block = points // grp
    for k in range(others):
        other = refs.pop(0)[...]
        cut = (others - k) * block
        mapped = mapped + jnp.concatenate([other[:, cut:], other[:, :cut]], axis=1)
    factor = refs.pop(0)[...][:, :modes] if has_factor else None
    weight = refs.pop(0)[:1]
    if has_factor:
        mapped = jnp.dot(factor, mapped, precision=HIGHEST, preferred_element_type=F32)
    mapped = mapped * weight / samples
    padded = jnp.concatenate([mapped, jnp.zeros((LANES - modes, points), F32)], axis=0)
    gram = lax.dot_general(
        mapped, padded, (((1,), (1,)), ((), ())), precision=HIGHEST, preferred_element_type=F32
    )
    tile = fold(gram, modes)
    if last:
        out_ref, send_ref = refs
        out_ref[...] = mapped[:, :block]
        slab = own_slab(tile, place, grp)
        for d in range(send_ref.shape[0]):
            send_ref[d] = slab
        return
    field_ref, send_ref = refs
    pitch = ROWS + 1
    store_tiles(send_ref, dot_wide(mapped * weight, field_ref[...]), pitch)
    for d in range(send_ref.shape[0] // pitch):
        send_ref[d * pitch + ROWS : (d + 1) * pitch] = tile[d % ROWS : d % ROWS + 1]


def finish_kernel(side_ref, recv_ref, mapped_ref, out_ref, *, grp, pts, points):
    total = whole_tile(lambda d: recv_ref[d], side_ref[0] * (grp * pts), grp, pts)
    mapped = mapped_ref[...]
    modes = mapped.shape[0]
    factor = inverse_factor(unfold(total, modes) / points, modes)[:, :modes]
    out_ref[...] = jnp.dot(factor, mapped, precision=HIGHEST, preferred_element_type=F32)


def call(kernel, outs, *args):
    specs = [SMEM if a.dtype == jnp.int32 else VMEM for a in args]
    args = [
        a if a.dtype == jnp.int32 else pltpu.with_memory_space_constraint(a, pltpu.VMEM)
        for a in args
    ]
    out = [o if isinstance(o, jax.ShapeDtypeStruct) else pltpu.VMEM(*o) for o in outs]
    result = pl.pallas_call(
        kernel,
        out_shape=out,
        in_specs=specs,
        out_specs=[VMEM for _ in out],
        compiler_params=GRANT,
    )(*args)
    return result if len(out) > 1 else result[0]


def begin(place, side, fields, weight, modes, grp):
    _, points, samples = fields.shape
    columns, rows, far = samples // grp, modes.shape[1], pl.BlockSpec(memory_space=pltpu.HBM)
    fields, weight, modes = (
        pltpu.with_memory_space_constraint(a, pltpu.HBM) for a in (fields, weight, modes)
    )
    out = [pltpu.VMEM((ROWS, points), F32), pltpu.VMEM((rows, points), F32)]
    out += [pltpu.VMEM((rows + ROWS, columns), F32) for _ in range(1, grp)]
    out += [pltpu.VMEM((points, columns), fields.dtype) for _ in range(1, grp)]
    weights, weighted, *rest = pl.pallas_call(
        send_kernel,
        out_shape=out,
        in_specs=[SMEM, SMEM, far, far, far],
        out_specs=[VMEM for _ in out],
        compiler_params=GRANT,
        scratch_shapes=[
            pltpu.VMEM((1, points), F32),
            pltpu.VMEM((rows, points), F32),
            pltpu.SemaphoreType.DMA((grp + 1,)),
        ],
    )(place, side, fields, weight, modes)
    part, block = pl.pallas_call(
        lambda *refs: keep_kernel(*refs, grp=grp),
        out_shape=[pltpu.VMEM((rows, columns), F32), pltpu.VMEM((points, columns), BF16)],
        in_specs=[SMEM, VMEM, far],
        out_specs=[VMEM, VMEM],
        compiler_params=GRANT,
        scratch_shapes=[pltpu.SemaphoreType.DMA],
    )(place, pltpu.with_memory_space_constraint(weighted, pltpu.VMEM), fields)
    return weights, part, rest[: grp - 1], [block] + rest[grp - 1 :]


def exchange(value, pitch=None):
    if pitch is None:
        return lax.all_to_all(value, ALL, 0, 0)
    chunks = value.shape[0] // pitch
    unit = ROWS if pitch == ROWS else 1
    split = value.reshape(chunks, pitch // unit, unit, LANES)
    return lax.all_to_all(split, ALL, 0, 0).reshape(value.shape)


def shifted(value, shift):
    grp = lax.axis_size("grp")
    return lax.ppermute(value, "grp", [((i + shift) % grp, i) for i in range(grp)])


def body_tiles(fields, point_weight, start_modes):
    modes, samples = start_modes.shape[1], fields.shape[2]
    grp, pts = lax.axis_size("grp"), lax.axis_size("pts")
    devices = 2 * grp * pts
    total_points = fields.shape[1] * grp * pts
    points = fields.shape[1] * grp
    place = lax.axis_index("grp").astype(jnp.int32).reshape(1)
    side = lax.axis_index("side").astype(jnp.int32).reshape(1)

    weights, part, messages, blocks = begin(
        place, side, fields, point_weight, start_modes, grp
    )
    messages = [shifted(m, k + 1) for k, m in enumerate(messages)]
    *others, part = lax.optimization_barrier((*blocks[1:], part))
    blocks = [blocks[0]] + [shifted(block, k + 1) for k, block in enumerate(others)]
    pitch = ROWS
    outs = [((devices * ROWS, LANES), F32), ((ROWS, points), F32)]
    send, weight = call(first_kernel, outs, weights, part, *messages)
    for iteration in range(ITERS):
        has_gram, last = iteration > 0, iteration == ITERS - 1
        kernel = lambda *refs: reduce_kernel(*refs, grp=grp, pts=pts, pitch=pitch)
        dtype = F32 if has_gram else BF16
        summed = call(kernel, [((devices * pitch, LANES), dtype)], exchange(send, pitch))
        if not has_gram:
            summed, *blocks = lax.optimization_barrier((summed, *blocks))
        gathered = exchange(summed, pitch)
        outs = [((modes, points), F32)]
        if has_gram:
            kernel = lambda *refs: back_kernel(*refs, pitch=pitch)
            own = call(kernel, outs, gathered, turned)
            kernel = lambda *refs: factor_kernel(
                *refs, modes=modes, points=total_points, pitch=pitch
            )
            factor = [call(kernel, [((modes, LANES), F32)], gathered)]
        else:
            own = call(first_back_kernel, outs, gathered, *blocks)
            outs = [((points, samples // grp), BF16), ((samples // grp, points), BF16)]
            field, turned = call(join_kernel, outs, own, *blocks)
            factor = []
        others = [shifted(own, k) for k in range(1, grp)]
        pitch = ROWS + 1
        kernel = lambda *refs: map_kernel(
            *refs, samples=samples, others=grp - 1, has_factor=has_gram, last=last
        )
        given = [place, own, *others, *factor, weight]
        if last:
            outs = [((modes, points // grp), F32), ((devices, ROWS // grp, LANES), F32)]
            mapped, send = call(kernel, outs, *given)
        else:
            send = call(kernel, [((devices * pitch, LANES), F32)], *given, field)
    kernel = lambda *refs: finish_kernel(*refs, grp=grp, pts=pts, points=total_points)
    out = jax.ShapeDtypeStruct((modes, points // grp), F32)
    return call(kernel, [out], side, exchange(send), mapped)[None]


def body_sums(fields, point_weight, start_modes):
    local_field, weight, mode_rows = fields[0], point_weight[0], start_modes[0]
    samples = local_field.shape[1]
    total_points = local_field.shape[0] * lax.axis_size("grp") * lax.axis_size("pts")
    for _ in range(ITERS):
        weighted = (mode_rows * weight[None, :]).astype(BF16)
        partial = jnp.dot(weighted, local_field, preferred_element_type=F32)
        coeffs = lax.psum(partial, ("grp", "pts")).astype(BF16)
        partner = lax.ppermute(coeffs, "side", [(0, 1), (1, 0)])
        mapped = lax.dot_general(
            partner, local_field, (((1,), (1,)), ((), ())), preferred_element_type=F32
        )
        mapped = mapped * weight[None, :] / samples
        gram = jnp.dot(mapped, mapped.T, precision=HIGHEST, preferred_element_type=F32)
        gram = lax.psum(gram, ("grp", "pts")) / total_points
        factor = jnp.linalg.cholesky(gram)
        mode_rows = lax.linalg.triangular_solve(factor, mapped, left_side=True, lower=True)
    return mode_rows[None]


def solution(mesh):
    grp, pts = mesh.shape["grp"], mesh.shape["pts"]

    def run(fields, point_weight, start_modes):
        modes, samples = start_modes.shape[1], fields.shape[2]
        tiles = (modes // ROWS) * (samples // (LANES * grp))
        fits = tiles == 2 * grp * pts and 4 * modes == LANES and ROWS % grp == 0
        fits = fits and fields.shape[1] <= samples * pts
        placed = (
            P("side", ("grp", "pts"), None),
            P("side", ("grp", "pts")),
            P("side", None, ("grp", "pts")),
        )
        return jax.shard_map(
            body_tiles if fits else body_sums,
            mesh=mesh,
            in_specs=placed,
            out_specs=P("side", None, ("grp", "pts")),
            check_vma=False,
        )(fields, point_weight, start_modes)

    return run
```

```python
import jax
import jax.numpy as jnp
from jax import lax
from jax.experimental import pallas as pl
from jax.experimental.pallas import tpu as pltpu
from jax.sharding import PartitionSpec as P

ITERS = 6
ROWS, LANES = 8, 128
ALL = ("side", "grp", "pts")
F32, BF16 = jnp.float32, jnp.bfloat16
HIGHEST = lax.Precision.HIGHEST
VMEM = pl.BlockSpec(memory_space=pltpu.VMEM)
SMEM = pl.BlockSpec(memory_space=pltpu.SMEM)
GRANT = pltpu.CompilerParams(vmem_limit_bytes=8 << 20)


def split3(x):
    high = x.astype(BF16)
    rest = x - high.astype(F32)
    mid = rest.astype(BF16)
    low = (rest - mid.astype(F32)).astype(BF16)
    return jnp.concatenate([high, mid, low], axis=0)


def dot_wide(x, field):
    count = x.shape[0]
    out = jnp.dot(split3(x), field, preferred_element_type=F32)
    return out[2 * count :] + out[count : 2 * count] + out[:count]


def fold(gram, modes):
    return sum(
        pltpu.roll(gram[g * ROWS : (g + 1) * ROWS], g * modes, 1) if g else gram[:ROWS]
        for g in range(modes // ROWS)
    )


def unfold(tile, modes):
    lane = lax.broadcasted_iota(jnp.int32, (ROWS, LANES), 1)
    parts = [
        pltpu.roll(tile, LANES - g * modes, 1) if g else tile for g in range(modes // ROWS)
    ]
    return jnp.concatenate([jnp.where(lane < modes, part, 0.0) for part in parts], axis=0)


def inverse_factor(gram, modes):
    row = lax.broadcasted_iota(jnp.int32, (modes, LANES), 0)
    lane = lax.broadcasted_iota(jnp.int32, (modes, LANES), 1)
    work = gram + jnp.where(lane == row + modes, 1.0, 0.0)
    for k in range(0, modes, ROWS):
        rows = [work[k + j : k + j + 1] for j in range(ROWS)]
        columns = [
            jnp.broadcast_to(work[:, k + j : k + j + 1], (modes, LANES)) for j in range(ROWS)
        ]
        block = {
            (i, j): jnp.broadcast_to(rows[i][:, k + j : k + j + 1], (1, LANES))
            for i in range(ROWS)
            for j in range(i, ROWS)
        }
        factors = []
        for j in range(ROWS):
            inverse = 1.0 / block[j, j]
            factor = jnp.where(row > k + j, columns[j] * inverse, 0.0)
            factors.append(factor)
            for i in range(j + 1, ROWS):
                columns[i] = columns[i] - factor * block[j, i]
                ratio = block[j, i] * inverse
                for c in range(i, ROWS):
                    block[i, c] = block[i, c] - ratio * block[j, c]
                rows[i] = rows[i] - ratio * rows[j]
        for j in range(ROWS):
            work = work - factors[j] * rows[j]
    pivots = jnp.sum(jnp.where(lane == row, work, 0.0), axis=1, keepdims=True)
    inverse = pltpu.roll(work, LANES - modes, 1) / jnp.sqrt(pivots)
    return jnp.where(lane < modes, inverse, 0.0)


def store_tiles(send_ref, projected, pitch):
    columns = projected.shape[1] // LANES
    for d in range(send_ref.shape[0] // pitch):
        h, j = divmod(d, columns)
        send_ref[d * pitch : d * pitch + ROWS] = projected[
            h * ROWS : (h + 1) * ROWS, j * LANES : (j + 1) * LANES
        ]


def own_slab(tile, place, grp):
    slab = ROWS // grp
    return sum(
        jnp.where(place == c, tile[c * slab : (c + 1) * slab], 0.0) for c in range(grp)
    )


def whole_tile(read, first, grp, pts):
    slabs = []
    for c in range(grp):
        total = read(first + c * pts)
        for p in range(1, pts):
            total = total + read(first + c * pts + p)
        slabs.append(total)
    return jnp.concatenate(slabs, axis=0)


def own_part(place_ref, fields_ref, back, columns, grp):
    start = pl.multiple_of(lax.rem(place_ref[0] + grp - back, grp) * columns, LANES)
    return fields_ref.at[0, :, pl.ds(start, columns)]


def send_kernel(place_ref, _, fields_ref, weight_ref, modes_ref, weights_ref, weighted_ref, *rest):
    *out_refs, row_ref, modes_vmem, sems = rest
    others = len(out_refs) // 2
    message_refs, block_refs = out_refs[:others], out_refs[others:]
    modes = weighted_ref.shape[0]
    pairs = [(weight_ref, row_ref), (modes_ref.at[0], modes_vmem)]
    for k, ref in enumerate(block_refs):
        columns = ref.shape[1]
        back = (k + 1) % (others + 1)
        pairs.append((own_part(place_ref, fields_ref, back, columns, others + 1), ref))
    copies = [
        pltpu.make_async_copy(source, target, sems.at[i])
        for i, (source, target) in enumerate(pairs)
    ]
    for copy in copies:
        copy.start()
    copies[0].wait()
    copies[1].wait()
    weights = jnp.broadcast_to(row_ref[...], weights_ref.shape)
    weights_ref[...] = weights
    weighted = modes_vmem[...] * row_ref[...]
    weighted_ref[...] = weighted
    points = weights.shape[1]
    for message, block, copy in zip(message_refs, block_refs, copies[2:]):
        message[modes:, :points] = weights
        message[modes:, points:] = jnp.zeros((ROWS, message.shape[1] - points), F32)
        copy.wait()
        message[:modes] = dot_wide(weighted, block[...])
    copies[-1].wait()


def keep_kernel(weighted_ref, block_ref, part_ref):
    part_ref[...] = dot_wide(weighted_ref[...], block_ref[...])


def first_kernel(weights_ref, part_ref, *refs):
    *message_refs, send_ref, weight_ref = refs
    modes, points = part_ref.shape[0], weights_ref.shape[1]
    total, weights = part_ref[...], [weights_ref[...]]
    for ref in message_refs:
        total = total + ref[:modes]
        weights.append(ref[modes:, :points])
    store_tiles(send_ref, total, ROWS)
    weight_ref[...] = jnp.concatenate(weights, axis=1)


def reduce_kernel(recv_ref, send_ref, *, grp, pts, pitch):
    def total(first, rows):
        parts = [recv_ref[d * pitch + rows.start : d * pitch + rows.stop] for d in
                 range(first, first + pts)]
        return sum(parts[1:], parts[0])

    for s in range(2):
        gram = total(s * grp * pts, slice(ROWS, pitch)) if pitch > ROWS else None
        for c in range(grp):
            tile = total((s * grp + c) * pts, slice(0, ROWS)).astype(send_ref.dtype)
            for p in range(pts):
                first = (((1 - s) * grp + c) * pts + p) * pitch
                send_ref[first : first + ROWS] = tile
                if pitch > ROWS:
                    send_ref[first + ROWS : first + pitch] = gram


def factor_kernel(recv_ref, out_ref, *, modes, points, pitch):
    gram = jnp.concatenate(
        [recv_ref[r * pitch + ROWS : (r + 1) * pitch] for r in range(ROWS)], axis=0
    )
    out_ref[...] = inverse_factor(unfold(gram, modes) / points, modes)


def gathered_rows(recv_ref, columns, pitch):
    count = recv_ref.shape[0] // (pitch * columns)
    return jnp.concatenate(
        [
            jnp.concatenate(
                [
                    recv_ref[(h * columns + j) * pitch : (h * columns + j) * pitch + ROWS]
                    for j in range(columns)
                ],
                axis=1,
            )
            for h in range(count)
        ],
        axis=0,
    )


def first_back_kernel(recv_ref, *refs):
    *block_refs, out_ref = refs
    coeffs = gathered_rows(recv_ref, block_refs[0].shape[1] // LANES, ROWS)
    points = block_refs[0].shape[0]
    for k, ref in enumerate(block_refs):
        out_ref[:, k * points : (k + 1) * points] = lax.dot_general(
            coeffs, ref[...], (((1,), (1,)), ((), ())), preferred_element_type=F32
        )


def back_kernel(recv_ref, turned_ref, out_ref, *, pitch):
    coeffs = gathered_rows(recv_ref, turned_ref.shape[0] // LANES, pitch)
    out_ref[...] = dot_wide(coeffs, turned_ref[...])


def join_kernel(_, *refs):
    *block_refs, field_ref, turned_ref = refs
    points = block_refs[0].shape[0]
    for k, ref in enumerate(block_refs):
        field_ref[k * points : (k + 1) * points] = ref[...]
        turned_ref[:, k * points : (k + 1) * points] = ref[...].T


def map_kernel(*refs, samples, others, has_factor, last):
    refs = list(refs)
    place, grp = refs.pop(0)[0], others + 1
    mapped = refs.pop(0)[...]
    modes, points = mapped.shape
    block = points // grp
    for k in range(others):
        other = refs.pop(0)[...]
        cut = (others - k) * block
        mapped = mapped + jnp.concatenate([other[:, cut:], other[:, :cut]], axis=1)
    factor = refs.pop(0)[...][:, :modes] if has_factor else None
    weight = refs.pop(0)[:1]
    if has_factor:
        mapped = jnp.dot(factor, mapped, precision=HIGHEST, preferred_element_type=F32)
    mapped = mapped * weight / samples
    if not last:
        field_ref, send_ref = refs
        pitch = ROWS + 1
        store_tiles(send_ref, dot_wide(mapped * weight, field_ref[...]), pitch)
    padded = jnp.concatenate([mapped, jnp.zeros((LANES - modes, points), F32)], axis=0)
    gram = lax.dot_general(
        mapped, padded, (((1,), (1,)), ((), ())), precision=HIGHEST, preferred_element_type=F32
    )
    tile = fold(gram, modes)
    if last:
        out_ref, send_ref = refs
        out_ref[...] = mapped[:, :block]
        slab = own_slab(tile, place, grp)
        for d in range(send_ref.shape[0]):
            send_ref[d] = slab
        return
    for d in range(send_ref.shape[0] // pitch):
        send_ref[d * pitch + ROWS : (d + 1) * pitch] = tile[d % ROWS : d % ROWS + 1]


def finish_kernel(side_ref, recv_ref, mapped_ref, out_ref, *, grp, pts, points):
    total = whole_tile(lambda d: recv_ref[d], side_ref[0] * (grp * pts), grp, pts)
    mapped = mapped_ref[...]
    modes = mapped.shape[0]
    factor = inverse_factor(unfold(total, modes) / points, modes)[:, :modes]
    out_ref[...] = jnp.dot(factor, mapped, precision=HIGHEST, preferred_element_type=F32)


def call(kernel, outs, *args):
    specs = [SMEM if a.dtype == jnp.int32 else VMEM for a in args]
    args = [
        a if a.dtype == jnp.int32 else pltpu.with_memory_space_constraint(a, pltpu.VMEM)
        for a in args
    ]
    out = [o if isinstance(o, jax.ShapeDtypeStruct) else pltpu.VMEM(*o) for o in outs]
    result = pl.pallas_call(
        kernel,
        out_shape=out,
        in_specs=specs,
        out_specs=[VMEM for _ in out],
        compiler_params=GRANT,
    )(*args)
    return result if len(out) > 1 else result[0]


def begin(place, side, fields, weight, modes, grp):
    _, points, samples = fields.shape
    columns, rows, far = samples // grp, modes.shape[1], pl.BlockSpec(memory_space=pltpu.HBM)
    fields, weight, modes = (
        pltpu.with_memory_space_constraint(a, pltpu.HBM) for a in (fields, weight, modes)
    )
    out = [pltpu.VMEM((ROWS, points), F32), pltpu.VMEM((rows, points), F32)]
    out += [pltpu.VMEM((rows + ROWS, columns), F32) for _ in range(1, grp)]
    out += [pltpu.VMEM((points, columns), fields.dtype) for _ in range(grp)]
    weights, weighted, *rest = pl.pallas_call(
        send_kernel,
        out_shape=out,
        in_specs=[SMEM, SMEM, far, far, far],
        out_specs=[VMEM for _ in out],
        compiler_params=GRANT,
        scratch_shapes=[
            pltpu.VMEM((1, points), F32),
            pltpu.VMEM((rows, points), F32),
            pltpu.SemaphoreType.DMA((grp + 2,)),
        ],
    )(place, side, fields, weight, modes)
    messages, *blocks = rest[: grp - 1], *rest[grp - 1 :]
    blocks = [blocks[-1]] + blocks[:-1]
    part = call(keep_kernel, [((rows, columns), F32)], weighted, blocks[0])
    return weights, part, messages, blocks


def exchange(value, pitch=None):
    if pitch is None:
        return lax.all_to_all(value, ALL, 0, 0)
    chunks = value.shape[0] // pitch
    unit = ROWS if pitch == ROWS else 1
    split = value.reshape(chunks, pitch // unit, unit, LANES)
    return lax.all_to_all(split, ALL, 0, 0).reshape(value.shape)


def shifted(value, shift):
    grp = lax.axis_size("grp")
    return lax.ppermute(value, "grp", [((i + shift) % grp, i) for i in range(grp)])


def body_tiles(fields, point_weight, start_modes):
    modes, samples = start_modes.shape[1], fields.shape[2]
    grp, pts = lax.axis_size("grp"), lax.axis_size("pts")
    devices = 2 * grp * pts
    total_points = fields.shape[1] * grp * pts
    points = fields.shape[1] * grp
    place = lax.axis_index("grp").astype(jnp.int32).reshape(1)
    side = lax.axis_index("side").astype(jnp.int32).reshape(1)

    weights, part, messages, blocks = begin(
        place, side, fields, point_weight, start_modes, grp
    )
    messages = [shifted(m, k + 1) for k, m in enumerate(messages)]
    *others, part = lax.optimization_barrier((*blocks[1:], part))
    blocks = [blocks[0]] + [shifted(block, k + 1) for k, block in enumerate(others)]
    pitch = ROWS
    outs = [((devices * ROWS, LANES), F32), ((ROWS, points), F32)]
    send, weight = call(first_kernel, outs, weights, part, *messages)
    for iteration in range(ITERS):
        has_gram, last = iteration > 0, iteration == ITERS - 1
        kernel = lambda *refs: reduce_kernel(*refs, grp=grp, pts=pts, pitch=pitch)
        dtype = F32 if has_gram else BF16
        summed = call(kernel, [((devices * pitch, LANES), dtype)], exchange(send, pitch))
        if not has_gram:
            summed, *blocks = lax.optimization_barrier((summed, *blocks))
        gathered = exchange(summed, pitch)
        outs = [((modes, points), F32)]
        if has_gram:
            kernel = lambda *refs: back_kernel(*refs, pitch=pitch)
            own = call(kernel, outs, gathered, turned)
            kernel = lambda *refs: factor_kernel(
                *refs, modes=modes, points=total_points, pitch=pitch
            )
            factor = [call(kernel, [((modes, LANES), F32)], gathered)]
        else:
            own = call(first_back_kernel, outs, gathered, *blocks)
            outs = [((points, samples // grp), BF16), ((samples // grp, points), BF16)]
            field, turned = call(join_kernel, outs, own, *blocks)
            factor = []
        others = [shifted(own, k) for k in range(1, grp)]
        pitch = ROWS + 1
        kernel = lambda *refs: map_kernel(
            *refs, samples=samples, others=grp - 1, has_factor=has_gram, last=last
        )
        given = [place, own, *others, *factor, weight]
        if last:
            outs = [((modes, points // grp), F32), ((devices, ROWS // grp, LANES), F32)]
            mapped, send = call(kernel, outs, *given)
        else:
            send = call(kernel, [((devices * pitch, LANES), F32)], *given, field)
    kernel = lambda *refs: finish_kernel(*refs, grp=grp, pts=pts, points=total_points)
    out = jax.ShapeDtypeStruct((modes, points // grp), F32)
    return call(kernel, [out], side, exchange(send), mapped)[None]


def body_sums(fields, point_weight, start_modes):
    local_field, weight, mode_rows = fields[0], point_weight[0], start_modes[0]
    samples = local_field.shape[1]
    total_points = local_field.shape[0] * lax.axis_size("grp") * lax.axis_size("pts")
    for _ in range(ITERS):
        weighted = (mode_rows * weight[None, :]).astype(BF16)
        partial = jnp.dot(weighted, local_field, preferred_element_type=F32)
        coeffs = lax.psum(partial, ("grp", "pts")).astype(BF16)
        partner = lax.ppermute(coeffs, "side", [(0, 1), (1, 0)])
        mapped = lax.dot_general(
            partner, local_field, (((1,), (1,)), ((), ())), preferred_element_type=F32
        )
        mapped = mapped * weight[None, :] / samples
        gram = jnp.dot(mapped, mapped.T, precision=HIGHEST, preferred_element_type=F32)
        gram = lax.psum(gram, ("grp", "pts")) / total_points
        factor = jnp.linalg.cholesky(gram)
        mode_rows = lax.linalg.triangular_solve(factor, mapped, left_side=True, lower=True)
    return mode_rows[None]


def solution(mesh):
    grp, pts = mesh.shape["grp"], mesh.shape["pts"]

    def run(fields, point_weight, start_modes):
        modes, samples = start_modes.shape[1], fields.shape[2]
        tiles = (modes // ROWS) * (samples // (LANES * grp))
        fits = tiles == 2 * grp * pts and 4 * modes == LANES and ROWS % grp == 0
        fits = fits and fields.shape[1] <= samples * pts
        placed = (
            P("side", ("grp", "pts"), None),
            P("side", ("grp", "pts")),
            P("side", None, ("grp", "pts")),
        )
        return jax.shard_map(
            body_tiles if fits else body_sums,
            mesh=mesh,
            in_specs=placed,
            out_specs=P("side", None, ("grp", "pts")),
            check_vma=False,
        )(fields, point_weight, start_modes)

    return run
```
